32 devices in a mesh: grp: 2 (over y), row: 4 (over z), col: 4 (over x, core).
Axes of the slice: x: 2, y: 2, z: 4, core: 2. Of those that a mesh axis runs over, the one named last changes fastest.
Arguments:
- embedding: bfloat16 [4096, 512], P(('grp', 'row', 'col')), parts along dimension 0, may hold values from -3 to 3
- item_bias: bfloat16 [4096], P(('grp', 'row', 'col')), parts along dimension 0, may hold values from 0.5 to 2.5
- counts: int32 [8, 4, 12, 128, 128], P(('grp', 'row'), 'col'), parts along dimension 0, may hold values from 0 to 4096
- block_row: int32 [8, 4, 12], P(('grp', 'row'), 'col'), parts along dimension 0, may hold values from 0 to 3, as said below
- block_col: int32 [8, 4, 12], P(('grp', 'row'), 'col'), parts along dimension 0, may hold values from 0 to 3
- block_count: int32 [8, 4], P(('grp', 'row'), 'col'), parts along dimension 0, may hold values from 1 to 12, as said below
Outputs:
- grad_emb: float32 [4096, 512], P(('grp', 'row', 'col')), parts along dimension 0
- grad_bias: float32 [4096], P(('grp', 'row', 'col')), parts along dimension 0
The draws below stay inside these ranges and needn't reach their ends.
There are 2 independent parts, one for each index of `grp`. The reference program is written for one: setup_inputs(seed, part) draws one part's arguments, and reference() takes and returns one part's arrays. A program takes and returns all parts, laid end to end along the dimension named above; each array names one. Nothing has to cross between parts.
Inputs may be any that keep to these rules, and one draw needn't show every extreme that they name: Slots at or beyond block_count of a tile are unused; some tile lists all 12 slots. The listed positions (block_row, block_col) of one tile are distinct.
All inputs are finite; a program needn't handle non-finite values.
Results may differ from the reference program's by a relative error of at most 0.0075.
Values may be sent and summed in bfloat16 or wider, within the bound.
A program may use at most 64 MiB of HBM per device.

```python
import jax
import jax.numpy as jnp
from jax import lax

D = 512
BS = 128
ROWB = 4
ITEM_DEV = 128
COLB = 4
BLK_DEV = 12
ITEMS = 2048
N_ROW = 4
N_COL = 4


def listed_positions(key):
    layout_key = jax.random.fold_in(key, 7)
    tile_keys = jax.random.split(layout_key, N_ROW * N_COL)
    orders = jax.vmap(lambda single: jax.random.permutation(single, ROWB * COLB))(tile_keys)
    return orders[:, :BLK_DEV].reshape(N_ROW, N_COL, BLK_DEV).astype(jnp.int32)


def draw_block_row(key, part):
    return (listed_positions(key) // COLB).astype(jnp.int32)


def draw_block_col(key, part):
    return (listed_positions(key) % COLB).astype(jnp.int32)


def draw_block_count(key, part):
    shift_key, full_key = jax.random.split(jax.random.fold_in(key, 11))
    shifts = jax.random.randint(shift_key, (N_ROW, N_COL), 0, 4)
    listed = jnp.maximum(jnp.right_shift(jnp.full((N_ROW, N_COL), BLK_DEV, jnp.int32), shifts), 1)
    chosen = jax.random.randint(full_key, (), 0, N_ROW * N_COL)
    flat = listed.reshape(-1).at[chosen].set(BLK_DEV)
    return flat.reshape(N_ROW, N_COL).astype(jnp.int32)


def draw_counts(key, part):
    shape = (N_ROW, N_COL, BLK_DEV, BS, BS)
    power_key, value_key, zero_key = jax.random.split(jax.random.fold_in(key, 13), 3)
    powers = jax.random.randint(power_key, shape, 0, 13)
    upper = jnp.left_shift(jnp.ones(shape, jnp.int32), powers) + 1
    values = jax.random.randint(value_key, shape, 1, upper)
    keep = jax.random.randint(zero_key, shape, 0, 3) > 0
    return jnp.where(keep, values, 0).astype(jnp.int32)


def level_of(key, dims, cuts, least, high):
    factor_of, own = 1.0, jax.random.fold_in(key, 6)
    for dim, shards_of in cuts:
        steps = jnp.exp(jax.random.uniform(jax.random.fold_in(own, dim), (shards_of,), jnp.float32, least / len(cuts), high / len(cuts)))
        factor_of = factor_of * jnp.repeat(steps, dims[dim] // shards_of).reshape([-1 if axis == dim else 1 for axis in range(len(dims))])
    return factor_of


def normal_values(rng, dims, scale, limit, pieces=(), kind=jnp.bfloat16):
    result = scale * jax.random.normal(rng, dims, jnp.float32)
    if pieces:
        result = result * level_of(rng, dims, pieces, -0.22, 0.18)
    return jnp.clip(result, -limit, limit).astype(kind)


def setup_inputs(seed: int = 0, part: int = 0) -> dict:
    splits = jax.random.split(jax.random.key(seed), 7)
    part_keys = jax.random.split(jax.random.fold_in(splits[6], part), 7)
    return {
        "embedding": normal_values(part_keys[0], (ITEMS, D), (D ** -0.25), 3.0, ((0, 16),)),
        "item_bias": jnp.clip(0.5 + 2.0 * jax.random.uniform(part_keys[1], (ITEMS,), jnp.float32) ** level_of(part_keys[1], (ITEMS,), ((0, 16),), -0.2, 0.2), 0.5, 2.5).astype(jnp.bfloat16),
        "counts": draw_counts(jax.random.fold_in(jax.random.fold_in(splits[6], part), 71), part),
        "block_row": draw_block_row(jax.random.fold_in(jax.random.fold_in(splits[6], part), 71), part),
        "block_col": draw_block_col(jax.random.fold_in(jax.random.fold_in(splits[6], part), 71), part),
        "block_count": draw_block_count(jax.random.fold_in(jax.random.fold_in(splits[6], part), 71), part),
    }


def block_residual(row_rows, row_shift, col_rows, col_shift, tallies):
    scores = jnp.dot(row_rows, col_rows.T, preferred_element_type=jnp.float32)
    scores = scores + row_shift.astype(jnp.float32)[:, None] + col_shift.astype(jnp.float32)[None, :]
    floats = tallies.astype(jnp.float32)
    logged = jnp.log(jnp.maximum(floats, 1.0))
    weights = jnp.where(tallies > 0, jnp.minimum(1.0, jnp.exp(0.75 * (logged - jnp.log(100.0)))), 0.0)
    return weights * (scores - logged)


def block_grads(weighted, row_rows, col_rows):
    rounded = weighted.astype(jnp.bfloat16)
    to_rows = jnp.dot(rounded, col_rows, preferred_element_type=jnp.float32)
    to_cols = lax.dot_general(rounded, row_rows, (((0,), (0,)), ((), ())), preferred_element_type=jnp.float32)
    return to_rows, to_cols


def reference(embedding, item_bias, counts, block_row, block_col, block_count):
    width = embedding.shape[1]
    row_span = ROWB * BS
    col_span = COLB * BS
    spans = jnp.arange(col_span, dtype=jnp.int32)
    start_state = (jnp.zeros((ITEMS, width), jnp.float32), jnp.zeros((ITEMS, width), jnp.float32),
                   jnp.zeros((ITEMS,), jnp.float32), jnp.zeros((ITEMS,), jnp.float32))

    def tile(position, state):
        row_total, col_total, row_bias_total, col_bias_total = state
        position = jnp.asarray(position).astype(jnp.int32)
        grid_row = position // N_COL
        grid_col = position % N_COL
        row_base = (grid_row * (N_COL * ITEM_DEV)).astype(jnp.int32)
        row_rows = lax.dynamic_slice_in_dim(embedding, row_base, row_span, 0)
        row_shift = lax.dynamic_slice_in_dim(item_bias, row_base, row_span, 0)
        col_index = ((spans // ITEM_DEV) * (N_COL * ITEM_DEV) + grid_col * ITEM_DEV + spans % ITEM_DEV).astype(jnp.int32)
        col_rows = jnp.take(embedding, col_index, axis=0)
        col_shift = jnp.take(item_bias, col_index)
        listed = block_count[grid_row, grid_col]

        def block(slot, sums):
            slot = jnp.asarray(slot).astype(jnp.int32)

            def active(kept):
                row_acc, row_bacc, col_acc, col_bacc = kept
                row_start = (block_row[grid_row, grid_col, slot] * BS).astype(jnp.int32)
                col_start = (block_col[grid_row, grid_col, slot] * BS).astype(jnp.int32)
                block_rrows = lax.dynamic_slice_in_dim(row_rows, row_start, BS, 0)
                block_rshift = lax.dynamic_slice_in_dim(row_shift, row_start, BS, 0)
                block_crows = lax.dynamic_slice_in_dim(col_rows, col_start, BS, 0)
                block_cshift = lax.dynamic_slice_in_dim(col_shift, col_start, BS, 0)
                weighted = block_residual(block_rrows, block_rshift, block_crows, block_cshift,
                                          counts[grid_row, grid_col, slot])
                to_rows, to_cols = block_grads(weighted, block_rrows, block_crows)
                row_acc = lax.dynamic_update_slice_in_dim(
                    row_acc, lax.dynamic_slice_in_dim(row_acc, row_start, BS, 0) + to_rows, row_start, 0)
                row_bacc = lax.dynamic_update_slice_in_dim(
                    row_bacc, lax.dynamic_slice_in_dim(row_bacc, row_start, BS, 0) + jnp.sum(weighted, axis=1), row_start, 0)
                col_acc = lax.dynamic_update_slice_in_dim(
                    col_acc, lax.dynamic_slice_in_dim(col_acc, col_start, BS, 0) + to_cols, col_start, 0)
                col_bacc = lax.dynamic_update_slice_in_dim(
                    col_bacc, lax.dynamic_slice_in_dim(col_bacc, col_start, BS, 0) + jnp.sum(weighted, axis=0), col_start, 0)
                return (row_acc, row_bacc, col_acc, col_bacc)

            return lax.cond(slot < listed, active, lambda kept: kept, sums)

        local_start = (jnp.zeros((row_span, width), jnp.float32), jnp.zeros((row_span,), jnp.float32),
                       jnp.zeros((col_span, width), jnp.float32), jnp.zeros((col_span,), jnp.float32))
        row_acc, row_bacc, col_acc, col_bacc = lax.fori_loop(0, BLK_DEV, block, local_start)
        row_total = lax.dynamic_update_slice_in_dim(
            row_total, lax.dynamic_slice_in_dim(row_total, row_base, row_span, 0) + row_acc, row_base, 0)
        row_bias_total = lax.dynamic_update_slice_in_dim(
            row_bias_total, lax.dynamic_slice_in_dim(row_bias_total, row_base, row_span, 0) + row_bacc, row_base, 0)
        col_round = lax.optimization_barrier(col_acc.astype(jnp.bfloat16)).astype(jnp.float32)
        col_bround = lax.optimization_barrier(col_bacc.astype(jnp.bfloat16)).astype(jnp.float32)
        col_total = col_total.at[col_index].add(col_round)
        col_bias_total = col_bias_total.at[col_index].add(col_bround)
        return (row_total, col_total, row_bias_total, col_bias_total)

    row_total, col_total, row_bias_total, col_bias_total = lax.fori_loop(0, N_ROW * N_COL, tile, start_state)
    grad_emb = (row_total + col_total) * 0.0625
    grad_bias = (row_bias_total + col_bias_total) * 0.015625
    return grad_emb, grad_bias
```

```python
import functools

import jax
import jax.numpy as jnp
from jax import lax
from jax.experimental import pallas as pl
from jax.experimental.pallas import tpu as pltpu
from jax.sharding import PartitionSpec as P

MESH = pl.DeviceIdType.MESH
EXTRA = 8


def bias_rows(bias, width):
    items = bias.shape[1]
    first = lax.broadcasted_iota(jnp.int32, (EXTRA, items), 0) == 0
    rows = jnp.where(first, jnp.broadcast_to(bias, (EXTRA, items)), 0.0)
    if width > items:
        rows = jnp.concatenate([rows, jnp.zeros((EXTRA, width - items), jnp.float32)], axis=1)
    return rows.astype(jnp.bfloat16)


def nearest(me, k, n):
    inner = jnp.minimum(me, n - 1 - me)
    half = (k + 1) // 2
    both = me + half if k % 2 else me - half
    low = (me < n - 1 - me).astype(jnp.int32)
    one_side = low * k + (1 - low) * (n - 1 - k)
    return jnp.where(k <= 2 * inner, both, one_side)


def kernel(
    n_row, n_col, emb_ref, bias_hbm, counts_ref, brow_hbm, bcol_hbm, bcount_hbm,
    grad_ref, gbias_ref,
    brow_ref, bcol_ref, bcount_ref, bias_ref, rows, cols, tally, weight, logs, shift, wrow, racc, row_out, col_out, row_in, col_in, col_own,
    local_sem, rs_send, rs_recv, cs_send, cs_recv, ro_send, ro_recv, co_send, co_recv,
    rs_pass, cs_pass, last_w,
):
    items, width = emb_ref.shape
    slots, side = counts_ref.shape[2], counts_ref.shape[3]
    me_r, me_c = lax.axis_index("row"), lax.axis_index("col")
    span = n_col * items
    n_rb = span // side
    n_cb = n_row * items // side
    group = side // items

    load_bias = pltpu.make_async_copy(bias_hbm, bias_ref, local_sem.at[3])
    load_bias.start()
    load_emb = pltpu.make_async_copy(emb_ref, cols.at[me_r, pl.ds(0, items)], local_sem.at[0])
    load_emb.start()
    load_own = pltpu.make_async_copy(emb_ref, rows.at[me_c, pl.ds(0, items)], local_sem.at[1])
    load_own.start()
    loads = [
        pltpu.make_async_copy(src, dst, local_sem.at[4 + i])
        for i, (src, dst) in enumerate(
            ((brow_hbm, brow_ref), (bcol_hbm, bcol_ref), (bcount_hbm, bcount_ref))
        )
    ]
    for load in loads:
        load.start()
    load_counts = pltpu.make_async_copy(counts_ref.at[0, 0], tally, local_sem.at[2])
    load_counts.start()

    barrier = pltpu.get_barrier_semaphore()
    has_up, has_down = me_r < n_row - 1, me_r > 0
    chips = n_col // 2
    core, chip = lax.rem(me_c, 2), me_c // 2
    beside = me_c + 1 - 2 * core
    away = [lax.rem(chip + k, chips) * 2 + core for k in range(1, chips)]

    def greet(axis, to):
        pl.semaphore_signal(barrier, inc=1, device_id={axis: to}, device_id_type=MESH)

    pl.when(has_up)(lambda: greet("row", me_r + 1))
    pl.when(has_down)(lambda: greet("row", me_r - 1))
    for to in away + [beside]:
        greet("col", to)
    load_bias.wait()
    packed = bias_rows(bias_ref[...].astype(jnp.float32), width)
    cols[me_r, items : items + EXTRA, :] = packed
    rows[me_c, items : items + EXTRA, :] = packed
    load_counts.wait()
    for load in loads:
        load.wait()
    listed = bcount_ref[0, 0]

    def position(p, carry):
        bi, bj = p // n_cb, lax.rem(p, n_cb)
        slot = jnp.int32(0)
        found = jnp.int32(0)
        for s in range(slots):
            hit = jnp.logical_and(
                jnp.logical_and(brow_ref[0, 0, s] == bi, bcol_ref[0, 0, s] == bj), s < listed
            )
            slot = jnp.where(hit, s, slot)
            found = jnp.where(hit, 1, found)
        x = tally[slot] * found
        logged = jnp.log(jnp.maximum(x.astype(jnp.float32), 1.0))
        w = jnp.where(
            x > 0, jnp.minimum(1.0, jnp.exp(0.75 * (logged - jnp.log(jnp.float32(100.0))))), 0.0
        )
        at = pl.ds(pl.multiple_of(bi * side, side), side)
        weight[bj, at, :] = w
        logs[bj, at, :] = logged
        return carry


    load_emb.wait()
    load_own.wait()
    beyond = has_up.astype(jnp.int32) + has_down.astype(jnp.int32)
    pl.semaphore_wait(barrier, beyond + len(away) + 1)

    sent = []

    def send(src, dst, send_sem, recv_sem, axis, to, when=None):
        copy = pltpu.make_async_remote_copy(
            src_ref=src, dst_ref=dst, send_sem=send_sem, recv_sem=recv_sem,
            device_id={axis: to}, device_id_type=MESH,
        )
        if when is None:
            copy.start()
        else:
            pl.when(when)(copy.start)
        sent.append((copy, when))

    halves = (pl.ds(0, items // 2), pl.ds(items // 2, items - items // 2 + EXTRA))
    for h in range(2):
        mine = cols.at[me_r, halves[h]]
        send(mine, mine, cs_send.at[0, h], cs_recv.at[me_r, h], "row", me_r + 1, has_up)
        send(mine, mine, cs_send.at[1, h], cs_recv.at[me_r, h], "row", me_r - 1, has_down)
    mine = rows.at[me_c]
    for to in away:
        send(mine, mine, rs_send.at[to], rs_recv.at[me_c], "col", to)
    send(mine, mine, rs_send.at[beside], rs_recv.at[me_c], "col", beside)
    lax.fori_loop(0, n_rb * n_cb, position, 0)

    def arrived(buf, sem, axis, slot):
        pltpu.make_async_remote_copy(
            src_ref=buf.at[slot], dst_ref=buf.at[slot], send_sem=sem.at[slot],
            recv_sem=sem.at[slot], device_id={axis: slot}, device_id_type=MESH,
        ).wait_recv()

    def take(ms, when=None):
        for h in range(2):
            for m in ms:
                piece = cols.at[m, halves[h]]
                landed = pltpu.make_async_remote_copy(
                    src_ref=piece, dst_ref=piece, send_sem=cs_pass.at[m, h],
                    recv_sem=cs_recv.at[m, h], device_id={"row": m}, device_id_type=MESH,
                )
                if when is None:
                    landed.wait_recv()
                else:
                    pl.when(when)(landed.wait_recv)
                to = me_r + 2 * (m < me_r).astype(jnp.int32) - 1
                ok = jnp.logical_and(to >= 0, to < n_row)
                if when is not None:
                    ok = jnp.logical_and(ok, when)
                send(piece, piece, cs_pass.at[m, h], cs_recv.at[m, h], "row", to, ok)

    early = 2 if group == 1 and n_cb == 4 else 0
    inner = jnp.logical_and(has_up, has_down)
    if early:
        take([nearest(me_r, k, n_row) for k in range(1, early + 1)])
    for m in away:
        arrived(rows, rs_recv, "col", m)
        send(rows.at[m], rows.at[m], rs_pass.at[m], rs_recv.at[m], "col", beside)
    arrived(rows, rs_recv, "col", beside)
    for m in away:
        arrived(rows, rs_recv, "col", m + 1 - 2 * core)
    top = (lax.broadcasted_iota(jnp.int32, (EXTRA, side), 0) == 0).astype(jnp.float32).astype(jnp.bfloat16)
    for i in range(n_col):
        shift[i * items : (i + 1) * items, :] = lax.dot_general(
            rows[i, items : items + EXTRA, 0:items], top,
            (((0,), (0,)), ((), ())), preferred_element_type=jnp.float32,
        )

    all_rows = jnp.concatenate([rows[i, 0:items, :] for i in range(n_col)], axis=0)
    me_g = me_r // group
    for k in range(n_cb):
        jb = nearest(me_g, k, n_cb)
        if k == 0:
            members = [me_g * group + lax.rem(me_r + t, group) for t in range(1, group)]
        else:
            members = [jb * group + t for t in range(group)]
        if early and k == 1:
            take([nearest(me_r, early + 1, n_row)], inner)
        elif early and k == early + 1:
            take(members, jnp.logical_not(inner))
        elif not early:
            take(members)
        block = jnp.concatenate([cols[jb * group + t, 0:items, :] for t in range(group)], axis=0)
        cshift = jnp.concatenate(
            [cols[jb * group + t, items : items + EXTRA, 0:items].astype(jnp.float32)[0:1] for t in range(group)],
            axis=1,
        )
        scores = lax.dot_general(
            all_rows, block, (((1,), (1,)), ((), ())), preferred_element_type=jnp.float32
        )
        weighted = weight[jb] * (scores + shift[...] + cshift - logs[jb])
        rounded = weighted.astype(jnp.bfloat16)
        to_cols = lax.dot_general(
            rounded, all_rows, (((0,), (0,)), ((), ())), preferred_element_type=jnp.float32
        )
        sums = jnp.sum(weighted, axis=0, keepdims=True)
        if k == 0:
            wrow[...] = weighted
        else:
            wrow[...] += weighted
        for t in range(group):
            to = jb * group + t
            part = to_cols[t * items : (t + 1) * items]
            part_sums = sums[:, t * items : (t + 1) * items]
            col_out[to, 0:items, :] = part.astype(jnp.bfloat16)
            col_out[to, items : items + EXTRA, :] = bias_rows(part_sums, width)
            if k == 0:
                if group == 1:
                    col_own[0:items, :] = part
                    col_own[items : items + 1, 0:items] = part_sums
                else:

                    @pl.when(to == me_r)
                    def _():
                        col_own[0:items, :] = part
                        col_own[items : items + 1, 0:items] = part_sums
        for m in members:
            send(col_out.at[m], col_in.at[me_r], co_send.at[m], co_recv.at[me_r], "row", m)
        if k == n_cb - 1:
            last_w[...] = rounded
            last_block = block
        else:
            to_rows = jnp.dot(rounded, block, preferred_element_type=jnp.float32)
            if k == 0:
                racc[...] = to_rows
            else:
                racc[...] += to_rows

    def row_terms(at):
        return racc[at, :] + jnp.dot(
            last_w[at, :], last_block, preferred_element_type=jnp.float32
        )

    def row_sums(i):
        at = pl.ds(pl.multiple_of(i * items, items), items)
        return jnp.sum(jnp.transpose(wrow[at, :]), axis=0, keepdims=True)

    across = [a + t * (1 - 2 * core) for a in away for t in (0, 1)]
    for to in across + [beside]:
        at = pl.ds(pl.multiple_of(to * items, items), items)
        row_out[to, 0:items, :] = row_terms(at).astype(jnp.bfloat16)
        row_out[to, items : items + EXTRA, :] = bias_rows(row_sums(to), width)
        send(row_out.at[to], row_in.at[me_c], ro_send.at[to], ro_recv.at[me_c], "col", to)

    at = pl.ds(pl.multiple_of(me_c * items, items), items)
    total = row_terms(at) + col_own[0:items, :]
    btotal = row_sums(me_c) + col_own[items : items + 1, 0:items]

    def added(total, btotal, buf, slot):
        return (
            total + buf[slot, 0:items, :].astype(jnp.float32),
            btotal + buf[slot, items : items + EXTRA, 0:items].astype(jnp.float32)[0:1],
        )

    for k in range(1, n_col):
        slot = lax.rem(me_c + n_col - k, n_col)
        arrived(row_in, ro_recv, "col", slot)
        total, btotal = added(total, btotal, row_in, slot)
    for k in range(1, n_row):
        slot = nearest(me_r, k, n_row)
        arrived(col_in, co_recv, "row", slot)
        total, btotal = added(total, btotal, col_in, slot)
    grad_ref[...] = total * 0.0625
    gbias_ref[...] = btotal * 0.015625
    for copy, when in sent:
        if when is None:
            copy.wait_send()
        else:
            pl.when(when)(copy.wait_send)


def body(n_row, n_col, embedding, item_bias, counts, block_row, block_col, block_count):
    items, width = embedding.shape
    slots, side = counts.shape[2], counts.shape[3]
    span, across = n_col * items, n_row * items // side
    vmem = pl.BlockSpec(memory_space=pltpu.VMEM)
    smem = pl.BlockSpec(memory_space=pltpu.SMEM)
    hbm = pl.BlockSpec(memory_space=pltpu.HBM)
    tall = items + EXTRA
    dma = pltpu.SemaphoreType.DMA
    keep = lambda x: pltpu.with_memory_space_constraint(x, pltpu.HBM)
    grad, gbias = pl.pallas_call(
        functools.partial(kernel, n_row, n_col),
        out_shape=(
            jax.ShapeDtypeStruct((items, width), jnp.float32),
            jax.ShapeDtypeStruct((1, items), jnp.float32),
        ),
        in_specs=[hbm] * 6,
        out_specs=(vmem, vmem),
        scratch_shapes=[
            pltpu.SMEM((1, 1, slots), jnp.int32),
            pltpu.SMEM((1, 1, slots), jnp.int32),
            pltpu.SMEM((1, 1), jnp.int32),
            pltpu.VMEM((1, items), jnp.bfloat16),
            pltpu.VMEM((n_col, tall, width), jnp.bfloat16),
            pltpu.VMEM((n_row, tall, width), jnp.bfloat16),
            pltpu.VMEM((slots, side, side), jnp.int32),
            pltpu.VMEM((across, span, side), jnp.float32),
            pltpu.VMEM((across, span, side), jnp.float32),
            pltpu.VMEM((span, side), jnp.float32),
            pltpu.VMEM((span, side), jnp.float32),
            pltpu.VMEM((span, width), jnp.float32),
            pltpu.VMEM((n_col, tall, width), jnp.bfloat16),
            pltpu.VMEM((n_row, tall, width), jnp.bfloat16),
            pltpu.VMEM((n_col, tall, width), jnp.bfloat16),
            pltpu.VMEM((n_row, tall, width), jnp.bfloat16),
            pltpu.VMEM((items + 8, width), jnp.float32),
            dma((7,)),
            dma((n_col,)), dma((n_col,)),
            dma((2, 2)), dma((n_row, 2)),
            dma((n_col,)), dma((n_col,)),
            dma((n_row,)), dma((n_row,)),
            dma((n_col,)), dma((n_row, 2)),
            pltpu.VMEM((span, side), jnp.bfloat16),
        ],
        compiler_params=pltpu.CompilerParams(
            collective_id=0, has_side_effects=True, vmem_limit_bytes=48 << 20
        ),
    )(
        keep(embedding), keep(item_bias.reshape(1, items)), keep(counts),
        block_row, block_col, block_count,
    )
    return grad, gbias.reshape(items)


PIECES = 4


def line_kernel(
    emb_hbm, bias_hbm, counts_hbm, brow_hbm, bcol_hbm, bcount_hbm,
    grad_ref, gbias_ref,
    brow_ref, bcol_ref, bcount_ref, bias_ref, rows, cols, row_bias, col_bias, tally, weight, logs, shift, wrow, wbuf, racc,
    col_out, col_in, relay, row_out, row_in, csum_out, csum_in, rsum_out, rsum_in,
    load_sem, e_send, e_pass, e_recv, eb_send, eb_pass, eb_recv, r_send, r_pass, r_recv, rb_send, rb_pass, rb_recv,
    co_send, co_recv, relay_send, relay_recv, ro_send, ro_recv, cs_send, cs_recv, rs_send, rs_recv,
):
    items, width = emb_hbm.shape
    slots, side = counts_hbm.shape[2], counts_hbm.shape[3]
    n_row, n_col = cols.shape[0], rows.shape[0] // items
    piece = items // PIECES
    me_r, me_c = lax.axis_index("row"), lax.axis_index("col")
    mate, opp, mir = me_r + 1 - 2 * lax.rem(me_r, 2), lax.rem(me_r + 2, n_row), n_row - 1 - me_r
    end = jnp.logical_or(me_r == 0, me_r == n_row - 1)
    inner = jnp.logical_not(end)
    core = lax.rem(me_c, 2)
    beside, across = me_c + 1 - 2 * core, lax.rem(me_c + 2, n_col)
    diag = across + 1 - 2 * core

    def part(i):
        return pl.ds(i * piece, piece)

    def row_at(m, i=0, height=items):
        return pl.ds(pl.multiple_of(m * items + i * piece, piece), height)

    load_bias = pltpu.make_async_copy(bias_hbm, bias_ref, load_sem.at[0])
    load_emb = pltpu.make_async_copy(emb_hbm, cols.at[me_r], load_sem.at[1])
    load_own = pltpu.make_async_copy(emb_hbm, rows.at[row_at(me_c)], load_sem.at[2])
    load_lists = [
        pltpu.make_async_copy(src, dst, load_sem.at[3 + i])
        for i, (src, dst) in enumerate(((brow_hbm, brow_ref), (bcol_hbm, bcol_ref), (bcount_hbm, bcount_ref)))
    ]
    load_counts = pltpu.make_async_copy(counts_hbm.at[0, 0], tally, load_sem.at[6])
    for load in [load_emb, load_own, load_bias] + load_lists + [load_counts]:
        load.start()

    barrier = pltpu.get_barrier_semaphore()

    def greet(axis, to):
        pl.semaphore_signal(barrier, inc=1, device_id={axis: to}, device_id_type=MESH)

    greet("row", mate)
    pl.when(inner)(lambda: greet("row", mir))
    greet("col", across)
    greet("col", beside)

    load_bias.wait()
    own_bias = jnp.broadcast_to(bias_ref[...].astype(jnp.float32), (EXTRA, items))
    row_bias[me_c] = own_bias
    col_bias[me_r] = own_bias
    load_emb.wait()
    load_own.wait()
    pl.semaphore_wait(barrier, 3 + inner.astype(jnp.int32))

    sent = []

    def remote(src, dst, send_sem, recv_sem, axis, to):
        return pltpu.make_async_remote_copy(
            src_ref=src, dst_ref=dst, send_sem=send_sem, recv_sem=recv_sem,
            device_id={axis: to}, device_id_type=MESH,
        )

    def send(src, dst, send_sem, recv_sem, axis, to, when=None):
        copy = remote(src, dst, send_sem, recv_sem, axis, to)
        if when is None:
            copy.start()
        else:
            pl.when(when)(copy.start)
        sent.append((copy, when))

    def landed(dst, recv_sem, axis):
        remote(dst, dst, recv_sem, recv_sem, axis, me_r if axis == "row" else me_c).wait_recv()

    def drain():
        for copy, when in sent:
            if when is None:
                copy.wait_send()
            else:
                pl.when(when)(copy.wait_send)
        sent.clear()

    for i in range(PIECES):
        own = cols.at[me_r, part(i)]
        send(own, own, e_send.at[0, i], e_recv.at[me_r, i], "row", mate)
        send(own, own, e_send.at[1, i], e_recv.at[me_r, i], "row", mir, inner)
        own = rows.at[row_at(me_c, i, piece)]
        send(own, own, r_send.at[i], r_recv.at[me_c, i], "col", across)
    own = rows.at[row_at(me_c)]
    send(own, own, r_send.at[PIECES], r_recv.at[me_c, 0], "col", beside)
    own = col_bias.at[me_r]
    send(own, own, eb_send.at[0], eb_recv.at[me_r], "row", mate)
    send(own, own, eb_send.at[1], eb_recv.at[me_r], "row", mir, inner)
    own = row_bias.at[me_c]
    send(own, own, rb_send.at[0], rb_recv.at[me_c], "col", across)
    send(own, own, rb_send.at[1], rb_recv.at[me_c], "col", beside)

    for load in load_lists + [load_counts]:
        load.wait()
    listed = bcount_ref[0, 0]
    code = [
        jnp.where(s < listed, brow_ref[0, 0, s] * n_row + bcol_ref[0, 0, s], -1) for s in range(slots)
    ]

    def position(p, carry):
        bi, bj = p // n_row, lax.rem(p, n_row)
        slot = jnp.int32(0)
        found = jnp.int32(0)
        for s in range(slots):
            hit = code[s] == p
            slot = jnp.where(hit, s, slot)
            found = jnp.where(hit, 1, found)
        x = tally[slot] * found
        logged = jnp.log(jnp.maximum(x.astype(jnp.float32), 1.0))
        w = jnp.where(
            x > 0, jnp.minimum(1.0, jnp.exp(0.75 * (logged - jnp.log(jnp.float32(100.0))))), 0.0
        )
        at = pl.ds(pl.multiple_of(bi * side, side), side)
        weight[bj, at, :] = w
        logs[bj, at, :] = logged
        return carry

    lax.fori_loop(0, n_col * n_row, position, 0)

    def came(m, i):
        landed(cols.at[m, part(i)], e_recv.at[m, i], "row")

    def hand(m, i, to):
        return remote(
            cols.at[m, part(i)], cols.at[m, part(i)], e_pass.at[m, i], e_recv.at[m, i], "row", to
        )

    def bias_came(m):
        landed(col_bias.at[m], eb_recv.at[m], "row")

    def bias_hand(m, to):
        return remote(col_bias.at[m], col_bias.at[m], eb_pass.at[m], eb_recv.at[m], "row", to)

    def later(copy, when):
        sent.append((copy, when))
        return copy

    outward = [[later(hand(m, i, mate), inner) for i in range(PIECES)] for m in (mir, opp)]
    inward = [later(hand(mate, i, mir), inner) for i in range(PIECES)]
    bias_outward = [later(bias_hand(m, mate), inner) for m in (mir, opp)]
    bias_inward = later(bias_hand(mate, mir), inner)
    to_relay = [
        later(remote(col_out.at[mir, part(i)], relay.at[part(i)], relay_send.at[i], relay_recv.at[i], "row", mate), end)
        for i in range(PIECES)
    ]
    from_relay = [
        later(remote(col_out.at[opp, part(i)], col_in.at[me_r, part(i)], co_send.at[opp, i], co_recv.at[me_r, i], "row", opp), inner)
        for i in range(PIECES)
    ]

    for i in range(PIECES):
        landed(rows.at[row_at(across, i, piece)], r_recv.at[across, i], "col")
        passed = rows.at[row_at(across, i, piece)]
        send(passed, passed, r_pass.at[i], r_recv.at[across, i], "col", beside)
        came(mate, i)

        @pl.when(inner)
        def _():
            inward[i].start()
            came(mir, i)
            outward[0][i].start()

    bias_came(mate)

    @pl.when(inner)
    def _():
        bias_inward.start()
        bias_came(mir)
        bias_outward[0].start()

    landed(row_bias.at[across], rb_recv.at[across], "col")
    send(row_bias.at[across], row_bias.at[across], rb_pass.at[0], rb_recv.at[across], "col", beside)
    landed(rows.at[row_at(beside)], r_recv.at[beside, 0], "col")
    landed(row_bias.at[beside], rb_recv.at[beside], "col")
    for i in range(PIECES):
        landed(rows.at[row_at(diag, i, piece)], r_recv.at[diag, i], "col")
    landed(row_bias.at[diag], rb_recv.at[diag], "col")

    top = (lax.broadcasted_iota(jnp.int32, (EXTRA, side), 0) == 0).astype(jnp.float32).astype(jnp.bfloat16)
    for m in range(n_col):
        shift[m * items : (m + 1) * items, :] = lax.dot_general(
            row_bias[m].astype(jnp.bfloat16), top,
            (((0,), (0,)), ((), ())), preferred_element_type=jnp.float32,
        )

    pick = lambda a, b: jnp.where(end, a, b)
    order = [mate, pick(me_r, mir), pick(opp, me_r), pick(mir, opp)]

    def residual(k):
        m = order[k]
        scores = lax.dot_general(
            rows[...], cols[m], (((1,), (1,)), ((), ())), preferred_element_type=jnp.float32
        )
        weighted = weight[m] * (scores + shift[...] + col_bias[m, 0:1, :] - logs[m])
        wbuf[k] = weighted.astype(jnp.bfloat16)
        if k == 0:
            wrow[...] = weighted
        else:
            wrow[...] += weighted
        csum_out[m] = jnp.broadcast_to(jnp.sum(weighted, axis=0, keepdims=True), (EXTRA, side))

    def to_cols(k):
        col_out[order[k]] = lax.dot_general(
            wbuf[k], rows[...], (((0,), (0,)), ((), ())), preferred_element_type=jnp.float32
        ).astype(jnp.bfloat16)

    def send_col(k, when=None):
        m = order[k]
        send(col_out.at[m], col_in.at[me_r], co_send.at[m, 0], co_recv.at[me_r, 0], "row", m, when)

    def send_csum(k, when=None):
        m = order[k]
        send(csum_out.at[m], csum_in.at[me_r], cs_send.at[m], cs_recv.at[me_r], "row", m, when)

    def relay_e(pieces):
        for i in pieces:
            came(opp, i)
            outward[1][i].start()

    residual(0)
    to_cols(0)
    send_col(0, end)
    send_csum(0)
    pl.when(inner)(lambda: relay_e((0, 1)))

    residual(1)
    to_cols(1)
    send_col(1, inner)
    send_csum(1, inner)
    pl.when(inner)(lambda: relay_e((2,)))

    @pl.when(end)
    def _():
        for i in range(PIECES):
            came(opp, i)
        bias_came(opp)

    residual(2)
    to_cols(2)
    send_col(2, end)
    send_csum(2, end)

    racc[...] = jnp.dot(
        jnp.concatenate([wbuf[0], wbuf[1]], axis=1),
        jnp.concatenate([cols[order[0]], cols[order[1]]], axis=0),
        preferred_element_type=jnp.float32,
    )

    @pl.when(inner)
    def _():
        relay_e((3,))
        bias_came(opp)
        bias_outward[1].start()

    send_col(0, inner)

    @pl.when(end)
    def _():
        for i in range(PIECES):
            came(mir, i)
        bias_came(mir)

    residual(3)
    send_csum(3)
    pair = jnp.concatenate([cols[order[2]], cols[order[3]]], axis=0)

    def row_terms(m):
        at = row_at(m)
        left = jnp.concatenate([wbuf[2, at, :], wbuf[3, at, :]], axis=1)
        return racc[at, :] + jnp.dot(left, pair, preferred_element_type=jnp.float32)

    def row_sums(m):
        return jnp.sum(jnp.transpose(wrow[row_at(m), :]), axis=0, keepdims=True)

    row_out[0] = row_terms(diag).astype(jnp.bfloat16)
    send(row_out.at[0], row_in.at[0], ro_send.at[0], ro_recv.at[0], "col", beside)
    row_out[1] = row_terms(beside).astype(jnp.bfloat16)
    send(row_out.at[1], row_in.at[1], ro_send.at[1], ro_recv.at[1], "col", beside)

    to_cols(3)

    @pl.when(end)
    def _():
        for copy in to_relay:
            copy.start()

    mine = row_terms(across)
    landed(row_in.at[0], ro_recv.at[0], "col")
    row_out[2] = (mine + row_in[0].astype(jnp.float32)).astype(jnp.bfloat16)
    send(row_out.at[2], row_in.at[2], ro_send.at[2], ro_recv.at[2], "col", across)
    for m in (diag, across, beside):
        rsum_out[m] = jnp.broadcast_to(row_sums(m), (EXTRA, items))
        send(rsum_out.at[m], rsum_in.at[me_c], rs_send.at[m], rs_recv.at[me_c], "col", m)
    grad_ref[...] = row_terms(me_c) + col_out[me_r].astype(jnp.float32)
    btotal = row_sums(me_c) + csum_out[me_r, 0:1, :]

    @pl.when(inner)
    def _():
        for i in range(PIECES):
            landed(relay.at[part(i)], relay_recv.at[i], "row")
            col_out[opp, part(i), :] = (
                col_out[opp, part(i), :].astype(jnp.float32) + relay[part(i), :].astype(jnp.float32)
            ).astype(jnp.bfloat16)
            from_relay[i].start()

    landed(row_in.at[1], ro_recv.at[1], "col")
    landed(col_in.at[mate], co_recv.at[mate, 0], "row")
    grad_ref[...] += row_in[1].astype(jnp.float32) + col_in[mate].astype(jnp.float32)
    for m in (mate, opp, mir):
        landed(csum_in.at[m], cs_recv.at[m], "row")
        btotal += csum_in[m, 0:1, :]
    for m in (beside, across, diag):
        landed(rsum_in.at[m], rs_recv.at[m], "col")
        btotal += rsum_in[m, 0:1, :]
    gbias_ref[...] = btotal * 0.015625
    landed(row_in.at[2], ro_recv.at[2], "col")
    grad_ref[...] += row_in[2].astype(jnp.float32)

    @pl.when(inner)
    def _():
        landed(col_in.at[mir], co_recv.at[mir, 0], "row")
        landed(col_in.at[opp], co_recv.at[opp, 0], "row")
        grad_ref[...] = (
            grad_ref[...] + col_in[mir].astype(jnp.float32) + col_in[opp].astype(jnp.float32)
        ) * 0.0625

    @pl.when(end)
    def _():
        for i in range(PIECES):
            landed(col_in.at[opp, part(i)], co_recv.at[opp, i], "row")
            grad_ref[part(i), :] = (
                grad_ref[part(i), :] + col_in[opp, part(i), :].astype(jnp.float32)
            ) * 0.0625

    drain()


def line_body(n_row, n_col, embedding, item_bias, counts, block_row, block_col, block_count):
    items, width = embedding.shape
    slots, side = counts.shape[2], counts.shape[3]
    span = n_col * items
    bf16, f32 = jnp.bfloat16, jnp.float32
    vmem = pl.BlockSpec(memory_space=pltpu.VMEM)
    hbm = pl.BlockSpec(memory_space=pltpu.HBM)
    dma = pltpu.SemaphoreType.DMA
    keep = lambda x: pltpu.with_memory_space_constraint(x, pltpu.HBM)
    grad, gbias = pl.pallas_call(
        line_kernel,
        out_shape=(
            jax.ShapeDtypeStruct((items, width), f32),
            jax.ShapeDtypeStruct((1, items), f32),
        ),
        in_specs=[hbm] * 6,
        out_specs=(vmem, vmem),
        scratch_shapes=[
            pltpu.SMEM((1, 1, slots), jnp.int32),
            pltpu.SMEM((1, 1, slots), jnp.int32),
            pltpu.SMEM((1, 1), jnp.int32),
            pltpu.VMEM((1, items), bf16),
            pltpu.VMEM((span, width), bf16),
            pltpu.VMEM((n_row, items, width), bf16),
            pltpu.VMEM((n_col, EXTRA, items), f32),
            pltpu.VMEM((n_row, EXTRA, items), f32),
            pltpu.VMEM((slots, side, side), jnp.int32),
            pltpu.VMEM((n_row, span, side), f32),
            pltpu.VMEM((n_row, span, side), f32),
            pltpu.VMEM((span, side), f32),
            pltpu.VMEM((span, side), f32),
            pltpu.VMEM((n_row, span, side), bf16),
            pltpu.VMEM((span, width), f32),
            pltpu.VMEM((n_row, items, width), bf16),
            pltpu.VMEM((n_row, items, width), bf16),
            pltpu.VMEM((items, width), bf16),
            pltpu.VMEM((3, items, width), bf16),
            pltpu.VMEM((3, items, width), bf16),
            pltpu.VMEM((n_row, EXTRA, items), f32),
            pltpu.VMEM((n_row, EXTRA, items), f32),
            pltpu.VMEM((n_col, EXTRA, items), f32),
            pltpu.VMEM((n_col, EXTRA, items), f32),
            dma((7,)),
            dma((2, PIECES)), dma((n_row, PIECES)), dma((n_row, PIECES)),
            dma((2,)), dma((n_row,)), dma((n_row,)),
            dma((PIECES + 1,)), dma((PIECES,)), dma((n_col, PIECES)),
            dma((2,)), dma((1,)), dma((n_col,)),
            dma((n_row, PIECES)), dma((n_row, PIECES)),
            dma((PIECES,)), dma((PIECES,)),
            dma((3,)), dma((3,)),
            dma((n_row,)), dma((n_row,)),
            dma((n_col,)), dma((n_col,)),
        ],
        compiler_params=pltpu.CompilerParams(
            collective_id=0, has_side_effects=True, vmem_limit_bytes=48 << 20
        ),
    )(
        keep(embedding), keep(item_bias.reshape(1, items)), keep(counts),
        keep(block_row), keep(block_col), block_count,
    )
    return grad, gbias.reshape(items)


def solution(mesh):
    placed = (
        P(("grp", "row", "col"), None),
        P(("grp", "row", "col")),
        P(("grp", "row"), "col", None, None, None),
        P(("grp", "row"), "col", None),
        P(("grp", "row"), "col", None),
        P(("grp", "row"), "col"),
    )

    def either(*args):
        n_row, n_col = mesh.shape["row"], mesh.shape["col"]
        line = n_row == 4 and n_col == 4 and args[0].shape[0] == args[2].shape[3]
        return (line_body if line else body)(n_row, n_col, *args)

    return jax.shard_map(
        either,
        mesh=mesh,
        in_specs=placed,
        out_specs=(P(("grp", "row", "col"), None), P(("grp", "row", "col"))),
        check_vma=False,
    )
```

```python
import functools

import jax
import jax.numpy as jnp
from jax import lax
from jax.experimental import pallas as pl
from jax.experimental.pallas import tpu as pltpu
from jax.sharding import PartitionSpec as P

MESH = pl.DeviceIdType.MESH
EXTRA = 8


def bias_rows(bias, width):
    items = bias.shape[1]
    first = lax.broadcasted_iota(jnp.int32, (EXTRA, items), 0) == 0
    rows = jnp.where(first, jnp.broadcast_to(bias, (EXTRA, items)), 0.0)
    if width > items:
        rows = jnp.concatenate([rows, jnp.zeros((EXTRA, width - items), jnp.float32)], axis=1)
    return rows.astype(jnp.bfloat16)


def nearest(me, k, n):
    inner = jnp.minimum(me, n - 1 - me)
    half = (k + 1) // 2
    both = me + half if k % 2 else me - half
    low = (me < n - 1 - me).astype(jnp.int32)
    one_side = low * k + (1 - low) * (n - 1 - k)
    return jnp.where(k <= 2 * inner, both, one_side)


def kernel(
    n_row, n_col, emb_ref, bias_hbm, counts_ref, brow_hbm, bcol_hbm, bcount_hbm,
    grad_ref, gbias_ref,
    brow_ref, bcol_ref, bcount_ref, bias_ref, rows, cols, tally, weight, logs, shift, wrow, racc, row_out, col_out, row_in, col_in, col_own,
    local_sem, rs_send, rs_recv, cs_send, cs_recv, ro_send, ro_recv, co_send, co_recv,
    rs_pass, cs_pass, last_w,
):
    items, width = emb_ref.shape
    slots, side = counts_ref.shape[2], counts_ref.shape[3]
    me_r, me_c = lax.axis_index("row"), lax.axis_index("col")
    span = n_col * items
    n_rb = span // side
    n_cb = n_row * items // side
    group = side // items

    load_bias = pltpu.make_async_copy(bias_hbm, bias_ref, local_sem.at[3])
    load_bias.start()
    load_emb = pltpu.make_async_copy(emb_ref, cols.at[me_r, pl.ds(0, items)], local_sem.at[0])
    load_emb.start()
    load_own = pltpu.make_async_copy(emb_ref, rows.at[me_c, pl.ds(0, items)], local_sem.at[1])
    load_own.start()
    loads = [
        pltpu.make_async_copy(src, dst, local_sem.at[4 + i])
        for i, (src, dst) in enumerate(
            ((brow_hbm, brow_ref), (bcol_hbm, bcol_ref), (bcount_hbm, bcount_ref))
        )
    ]
    for load in loads:
        load.start()
    load_counts = pltpu.make_async_copy(counts_ref.at[0, 0], tally, local_sem.at[2])
    load_counts.start()

    barrier = pltpu.get_barrier_semaphore()
    has_up, has_down = me_r < n_row - 1, me_r > 0
    chips = n_col // 2
    core, chip = lax.rem(me_c, 2), me_c // 2
    beside = me_c + 1 - 2 * core
    away = [lax.rem(chip + k, chips) * 2 + core for k in range(1, chips)]

    def greet(axis, to):
        pl.semaphore_signal(barrier, inc=1, device_id={axis: to}, device_id_type=MESH)

    pl.when(has_up)(lambda: greet("row", me_r + 1))
    pl.when(has_down)(lambda: greet("row", me_r - 1))
    for to in away + [beside]:
        greet("col", to)
    load_bias.wait()
    packed = bias_rows(bias_ref[...].astype(jnp.float32), width)
    cols[me_r, items : items + EXTRA, :] = packed
    rows[me_c, items : items + EXTRA, :] = packed
    load_counts.wait()
    for load in loads:
        load.wait()
    listed = bcount_ref[0, 0]

    def position(p, carry):
        bi, bj = p // n_cb, lax.rem(p, n_cb)
        slot = jnp.int32(0)
        found = jnp.int32(0)
        for s in range(slots):
            hit = jnp.logical_and(
                jnp.logical_and(brow_ref[0, 0, s] == bi, bcol_ref[0, 0, s] == bj), s < listed
            )
            slot = jnp.where(hit, s, slot)
            found = jnp.where(hit, 1, found)
        x = tally[slot] * found
        logged = jnp.log(jnp.maximum(x.astype(jnp.float32), 1.0))
        w = jnp.where(
            x > 0, jnp.minimum(1.0, jnp.exp(0.75 * (logged - jnp.log(jnp.float32(100.0))))), 0.0
        )
        at = pl.ds(pl.multiple_of(bi * side, side), side)
        weight[bj, at, :] = w
        logs[bj, at, :] = logged
        return carry


    load_emb.wait()
    load_own.wait()
    beyond = has_up.astype(jnp.int32) + has_down.astype(jnp.int32)
    pl.semaphore_wait(barrier, beyond + len(away) + 1)

    sent = []

    def send(src, dst, send_sem, recv_sem, axis, to, when=None):
        copy = pltpu.make_async_remote_copy(
            src_ref=src, dst_ref=dst, send_sem=send_sem, recv_sem=recv_sem,
            device_id={axis: to}, device_id_type=MESH,
        )
        if when is None:
            copy.start()
        else:
            pl.when(when)(copy.start)
        sent.append((copy, when))

    halves = (pl.ds(0, items // 2), pl.ds(items // 2, items - items // 2 + EXTRA))
    for h in range(2):
        mine = cols.at[me_r, halves[h]]
        send(mine, mine, cs_send.at[0, h], cs_recv.at[me_r, h], "row", me_r + 1, has_up)
        send(mine, mine, cs_send.at[1, h], cs_recv.at[me_r, h], "row", me_r - 1, has_down)
    mine = rows.at[me_c]
    for to in away:
        send(mine, mine, rs_send.at[to], rs_recv.at[me_c], "col", to)
    send(mine, mine, rs_send.at[beside], rs_recv.at[me_c], "col", beside)
    lax.fori_loop(0, n_rb * n_cb, position, 0)

    def arrived(buf, sem, axis, slot):
        pltpu.make_async_remote_copy(
            src_ref=buf.at[slot], dst_ref=buf.at[slot], send_sem=sem.at[slot],
            recv_sem=sem.at[slot], device_id={axis: slot}, device_id_type=MESH,
        ).wait_recv()

    def take(ms, when=None):
        for h in range(2):
            for m in ms:
                piece = cols.at[m, halves[h]]
                landed = pltpu.make_async_remote_copy(
                    src_ref=piece, dst_ref=piece, send_sem=cs_pass.at[m, h],
                    recv_sem=cs_recv.at[m, h], device_id={"row": m}, device_id_type=MESH,
                )
                if when is None:
                    landed.wait_recv()
                else:
                    pl.when(when)(landed.wait_recv)
                to = me_r + 2 * (m < me_r).astype(jnp.int32) - 1
                ok = jnp.logical_and(to >= 0, to < n_row)
                if when is not None:
                    ok = jnp.logical_and(ok, when)
                send(piece, piece, cs_pass.at[m, h], cs_recv.at[m, h], "row", to, ok)

    early = 2 if group == 1 and n_cb == 4 else 0
    inner = jnp.logical_and(has_up, has_down)
    if early:
        take([nearest(me_r, k, n_row) for k in range(1, early + 1)])
    for m in away:
        arrived(rows, rs_recv, "col", m)
        send(rows.at[m], rows.at[m], rs_pass.at[m], rs_recv.at[m], "col", beside)
    arrived(rows, rs_recv, "col", beside)
    for m in away:
        arrived(rows, rs_recv, "col", m + 1 - 2 * core)
    top = (lax.broadcasted_iota(jnp.int32, (EXTRA, side), 0) == 0).astype(jnp.float32).astype(jnp.bfloat16)
    for i in range(n_col):
        shift[i * items : (i + 1) * items, :] = lax.dot_general(
            rows[i, items : items + EXTRA, 0:items], top,
            (((0,), (0,)), ((), ())), preferred_element_type=jnp.float32,
        )

    all_rows = jnp.concatenate([rows[i, 0:items, :] for i in range(n_col)], axis=0)
    me_g = me_r // group
    for k in range(n_cb):
        jb = nearest(me_g, k, n_cb)
        if k == 0:
            members = [me_g * group + lax.rem(me_r + t, group) for t in range(1, group)]
        else:
            members = [jb * group + t for t in range(group)]
        if early and k == 1:
            take([nearest(me_r, early + 1, n_row)], inner)
        elif early and k == early + 1:
            take(members, jnp.logical_not(inner))
        elif not early:
            take(members)
        block = jnp.concatenate([cols[jb * group + t, 0:items, :] for t in range(group)], axis=0)
        cshift = jnp.concatenate(
            [cols[jb * group + t, items : items + EXTRA, 0:items].astype(jnp.float32)[0:1] for t in range(group)],
            axis=1,
        )
        scores = lax.dot_general(
            all_rows, block, (((1,), (1,)), ((), ())), preferred_element_type=jnp.float32
        )
        weighted = weight[jb] * (scores + shift[...] + cshift - logs[jb])
        rounded = weighted.astype(jnp.bfloat16)
        to_cols = lax.dot_general(
            rounded, all_rows, (((0,), (0,)), ((), ())), preferred_element_type=jnp.float32
        )
        sums = jnp.sum(weighted, axis=0, keepdims=True)
        if k == 0:
            wrow[...] = weighted
        else:
            wrow[...] += weighted
        for t in range(group):
            to = jb * group + t
            part = to_cols[t * items : (t + 1) * items]
            part_sums = sums[:, t * items : (t + 1) * items]
            col_out[to, 0:items, :] = part.astype(jnp.bfloat16)
            col_out[to, items : items + EXTRA, :] = bias_rows(part_sums, width)
            if k == 0:
                if group == 1:
                    col_own[0:items, :] = part
                    col_own[items : items + 1, 0:items] = part_sums
                else:

                    @pl.when(to == me_r)
                    def _():
                        col_own[0:items, :] = part
                        col_own[items : items + 1, 0:items] = part_sums
        for m in members:
            send(col_out.at[m], col_in.at[me_r], co_send.at[m], co_recv.at[me_r], "row", m)
        if k == n_cb - 1:
            last_w[...] = rounded
            last_block = block
        else:
            to_rows = jnp.dot(rounded, block, preferred_element_type=jnp.float32)
            if k == 0:
                racc[...] = to_rows
            else:
                racc[...] += to_rows

    def row_terms(at):
        return racc[at, :] + jnp.dot(
            last_w[at, :], last_block, preferred_element_type=jnp.float32
        )

    def row_sums(i):
        at = pl.ds(pl.multiple_of(i * items, items), items)
        return jnp.sum(jnp.transpose(wrow[at, :]), axis=0, keepdims=True)

    across = [a + t * (1 - 2 * core) for a in away for t in (0, 1)]
    for to in across + [beside]:
        at = pl.ds(pl.multiple_of(to * items, items), items)
        row_out[to, 0:items, :] = row_terms(at).astype(jnp.bfloat16)
        row_out[to, items : items + EXTRA, :] = bias_rows(row_sums(to), width)
        send(row_out.at[to], row_in.at[me_c], ro_send.at[to], ro_recv.at[me_c], "col", to)

    at = pl.ds(pl.multiple_of(me_c * items, items), items)
    total = row_terms(at) + col_own[0:items, :]
    btotal = row_sums(me_c) + col_own[items : items + 1, 0:items]

    def added(total, btotal, buf, slot):
        return (
            total + buf[slot, 0:items, :].astype(jnp.float32),
            btotal + buf[slot, items : items + EXTRA, 0:items].astype(jnp.float32)[0:1],
        )

    for k in range(1, n_col):
        slot = lax.rem(me_c + n_col - k, n_col)
        arrived(row_in, ro_recv, "col", slot)
        total, btotal = added(total, btotal, row_in, slot)
    for k in range(1, n_row):
        slot = nearest(me_r, k, n_row)
        arrived(col_in, co_recv, "row", slot)
        total, btotal = added(total, btotal, col_in, slot)
    grad_ref[...] = total * 0.0625
    gbias_ref[...] = btotal * 0.015625
    for copy, when in sent:
        if when is None:
            copy.wait_send()
        else:
            pl.when(when)(copy.wait_send)


def body(n_row, n_col, embedding, item_bias, counts, block_row, block_col, block_count):
    items, width = embedding.shape
    slots, side = counts.shape[2], counts.shape[3]
    span, across = n_col * items, n_row * items // side
    vmem = pl.BlockSpec(memory_space=pltpu.VMEM)
    smem = pl.BlockSpec(memory_space=pltpu.SMEM)
    hbm = pl.BlockSpec(memory_space=pltpu.HBM)
    tall = items + EXTRA
    dma = pltpu.SemaphoreType.DMA
    keep = lambda x: pltpu.with_memory_space_constraint(x, pltpu.HBM)
    grad, gbias = pl.pallas_call(
        functools.partial(kernel, n_row, n_col),
        out_shape=(
            jax.ShapeDtypeStruct((items, width), jnp.float32),
            jax.ShapeDtypeStruct((1, items), jnp.float32),
        ),
        in_specs=[hbm] * 6,
        out_specs=(vmem, vmem),
        scratch_shapes=[
            pltpu.SMEM((1, 1, slots), jnp.int32),
            pltpu.SMEM((1, 1, slots), jnp.int32),
            pltpu.SMEM((1, 1), jnp.int32),
            pltpu.VMEM((1, items), jnp.bfloat16),
            pltpu.VMEM((n_col, tall, width), jnp.bfloat16),
            pltpu.VMEM((n_row, tall, width), jnp.bfloat16),
            pltpu.VMEM((slots, side, side), jnp.int32),
            pltpu.VMEM((across, span, side), jnp.float32),
            pltpu.VMEM((across, span, side), jnp.float32),
            pltpu.VMEM((span, side), jnp.float32),
            pltpu.VMEM((span, side), jnp.float32),
            pltpu.VMEM((span, width), jnp.float32),
            pltpu.VMEM((n_col, tall, width), jnp.bfloat16),
            pltpu.VMEM((n_row, tall, width), jnp.bfloat16),
            pltpu.VMEM((n_col, tall, width), jnp.bfloat16),
            pltpu.VMEM((n_row, tall, width), jnp.bfloat16),
            pltpu.VMEM((items + 8, width), jnp.float32),
            dma((7,)),
            dma((n_col,)), dma((n_col,)),
            dma((2, 2)), dma((n_row, 2)),
            dma((n_col,)), dma((n_col,)),
            dma((n_row,)), dma((n_row,)),
            dma((n_col,)), dma((n_row, 2)),
            pltpu.VMEM((span, side), jnp.bfloat16),
        ],
        compiler_params=pltpu.CompilerParams(
            collective_id=0, has_side_effects=True, vmem_limit_bytes=48 << 20
        ),
    )(
        keep(embedding), keep(item_bias.reshape(1, items)), keep(counts),
        block_row, block_col, block_count,
    )
    return grad, gbias.reshape(items)


PIECES = 4


def line_kernel(
    emb_hbm, bias_hbm, counts_hbm, brow_hbm, bcol_hbm, bcount_hbm,
    grad_ref, gbias_ref,
    brow_ref, bcol_ref, bcount_ref, bias_ref, rows, cols, row_bias, col_bias, tally, weight, logs, shift, wrow, wbuf, racc,
    col_out, col_in, relay, row_out, row_in, csum_out, csum_in, rsum_out, rsum_in,
    load_sem, e_send, e_pass, e_recv, eb_send, eb_pass, eb_recv, r_send, r_pass, r_recv, rb_send, rb_pass, rb_recv,
    co_send, co_recv, relay_send, relay_recv, ro_send, ro_recv, cs_send, cs_recv, rs_send, rs_recv,
):
    items, width = emb_hbm.shape
    slots, side = counts_hbm.shape[2], counts_hbm.shape[3]
    n_row, n_col = cols.shape[0], rows.shape[0] // items
    piece = items // PIECES
    me_r, me_c = lax.axis_index("row"), lax.axis_index("col")
    mate, opp, mir = me_r + 1 - 2 * lax.rem(me_r, 2), lax.rem(me_r + 2, n_row), n_row - 1 - me_r
    end = jnp.logical_or(me_r == 0, me_r == n_row - 1)
    inner = jnp.logical_not(end)
    core = lax.rem(me_c, 2)
    beside, across = me_c + 1 - 2 * core, lax.rem(me_c + 2, n_col)
    diag = across + 1 - 2 * core

    def part(i):
        return pl.ds(i * piece, piece)

    def row_at(m, i=0, height=items):
        return pl.ds(pl.multiple_of(m * items + i * piece, piece), height)

    load_bias = pltpu.make_async_copy(bias_hbm, bias_ref, load_sem.at[0])
    load_emb = pltpu.make_async_copy(emb_hbm, cols.at[me_r], load_sem.at[1])
    load_own = pltpu.make_async_copy(emb_hbm, rows.at[row_at(me_c)], load_sem.at[2])
    load_lists = [
        pltpu.make_async_copy(src, dst, load_sem.at[3 + i])
        for i, (src, dst) in enumerate(((brow_hbm, brow_ref), (bcol_hbm, bcol_ref), (bcount_hbm, bcount_ref)))
    ]
    load_counts = pltpu.make_async_copy(counts_hbm.at[0, 0], tally, load_sem.at[6])
    for load in [load_emb, load_own, load_bias] + load_lists + [load_counts]:
        load.start()

    barrier = pltpu.get_barrier_semaphore()

    def greet(axis, to):
        pl.semaphore_signal(barrier, inc=1, device_id={axis: to}, device_id_type=MESH)

    greet("row", mate)
    pl.when(inner)(lambda: greet("row", mir))
    greet("col", across)
    greet("col", beside)

    load_bias.wait()
    own_bias = jnp.broadcast_to(bias_ref[...].astype(jnp.float32), (EXTRA, items))
    row_bias[me_c] = own_bias
    col_bias[me_r] = own_bias
    load_emb.wait()
    load_own.wait()
    pl.semaphore_wait(barrier, 3 + inner.astype(jnp.int32))

    sent = []

    def remote(src, dst, send_sem, recv_sem, axis, to):
        return pltpu.make_async_remote_copy(
            src_ref=src, dst_ref=dst, send_sem=send_sem, recv_sem=recv_sem,
            device_id={axis: to}, device_id_type=MESH,
        )

    def send(src, dst, send_sem, recv_sem, axis, to, when=None):
        copy = remote(src, dst, send_sem, recv_sem, axis, to)
        if when is None:
            copy.start()
        else:
            pl.when(when)(copy.start)
        sent.append((copy, when))

    def landed(dst, recv_sem, axis):
        remote(dst, dst, recv_sem, recv_sem, axis, me_r if axis == "row" else me_c).wait_recv()

    def drain(copies):
        for group, when in ((None, None), (end, end), (inner, inner)):
            these = [copy for copy, w in copies if w is group]
            if when is None:
                for copy in these:
                    copy.wait_send()
            elif these:

                @pl.when(when)
                def _():
                    for copy in these:
                        copy.wait_send()

    own = col_bias.at[me_r]
    send(own, own, eb_send.at[0], eb_recv.at[me_r], "row", mate)
    send(own, own, eb_send.at[1], eb_recv.at[me_r], "row", mir, inner)
    own = row_bias.at[me_c]
    send(own, own, rb_send.at[0], rb_recv.at[me_c], "col", across)
    send(own, own, rb_send.at[1], rb_recv.at[me_c], "col", beside)

    for i in range(PIECES):
        own = cols.at[me_r, part(i)]
        send(own, own, e_send.at[0, i], e_recv.at[me_r, i], "row", mate)
        send(own, own, e_send.at[1, i], e_recv.at[me_r, i], "row", mir, inner)
        own = rows.at[row_at(me_c, i, piece)]
        send(own, own, r_send.at[i], r_recv.at[me_c, i], "col", across)
    own = rows.at[row_at(me_c)]
    send(own, own, r_send.at[PIECES], r_recv.at[me_c, 0], "col", beside)

    for load in load_lists + [load_counts]:
        load.wait()
    listed = bcount_ref[0, 0]
    code = [
        jnp.where(s < listed, brow_ref[0, 0, s] * n_row + bcol_ref[0, 0, s], -1) for s in range(slots)
    ]

    def position(p, carry):
        bi, bj = p // n_row, lax.rem(p, n_row)
        slot = jnp.int32(0)
        found = jnp.int32(0)
        for s in range(slots):
            hit = code[s] == p
            slot = jnp.where(hit, s, slot)
            found = jnp.where(hit, 1, found)
        x = tally[slot] * found
        logged = jnp.log(jnp.maximum(x.astype(jnp.float32), 1.0))
        w = jnp.where(
            x > 0, jnp.minimum(1.0, jnp.exp(0.75 * (logged - jnp.log(jnp.float32(100.0))))), 0.0
        )
        at = pl.ds(pl.multiple_of(bi * side, side), side)
        weight[bj, at, :] = w
        logs[bj, at, :] = logged
        return carry

    lax.fori_loop(0, n_col * n_row, position, 0)

    def came(m, i):
        landed(cols.at[m, part(i)], e_recv.at[m, i], "row")

    def hand(m, i, to):
        return remote(
            cols.at[m, part(i)], cols.at[m, part(i)], e_pass.at[m, i], e_recv.at[m, i], "row", to
        )

    def bias_came(m):
        landed(col_bias.at[m], eb_recv.at[m], "row")

    def bias_hand(m, to):
        return remote(col_bias.at[m], col_bias.at[m], eb_pass.at[m], eb_recv.at[m], "row", to)

    def later(copy, when):
        sent.append((copy, when))
        return copy

    outward = [[later(hand(m, i, mate), inner) for i in range(PIECES)] for m in (mir, opp)]
    inward = [later(hand(mate, i, mir), inner) for i in range(PIECES)]
    bias_outward = [later(bias_hand(m, mate), inner) for m in (mir, opp)]
    bias_inward = later(bias_hand(mate, mir), inner)
    to_relay = [
        [
            later(remote(col_out.at[m, part(i)], relay.at[k, part(i)], relay_send.at[k, i], relay_recv.at[k, i], "row", mate), end)
            for i in range(PIECES)
        ]
        for k, m in enumerate((opp, mir))
    ]
    from_relay = [
        [
            later(remote(col_out.at[m, part(i)], col_in.at[me_r, part(i)], co_send.at[m, i], co_recv.at[me_r, i], "row", m), inner)
            for i in range(PIECES)
        ]
        for m in (mir, opp)
    ]

    for i in range(PIECES):
        came(mate, i)
        if i == 0:
            bias_came(mate)

        @pl.when(inner)
        def _():
            if i == 0:
                bias_inward.start()
            inward[i].start()
            came(mir, i)
            if i == 0:
                bias_came(mir)
                bias_outward[0].start()
            outward[0][i].start()

        if i == 0:
            landed(row_bias.at[across], rb_recv.at[across], "col")
            send(row_bias.at[across], row_bias.at[across], rb_pass.at[0], rb_recv.at[across], "col", beside)
        landed(rows.at[row_at(across, i, piece)], r_recv.at[across, i], "col")
        passed = rows.at[row_at(across, i, piece)]
        send(passed, passed, r_pass.at[i], r_recv.at[across, i], "col", beside)

    landed(rows.at[row_at(beside)], r_recv.at[beside, 0], "col")
    landed(row_bias.at[beside], rb_recv.at[beside], "col")
    for i in range(PIECES):
        landed(rows.at[row_at(diag, i, piece)], r_recv.at[diag, i], "col")
    landed(row_bias.at[diag], rb_recv.at[diag], "col")

    top = (lax.broadcasted_iota(jnp.int32, (EXTRA, side), 0) == 0).astype(jnp.float32).astype(jnp.bfloat16)
    for m in range(n_col):
        shift[m * items : (m + 1) * items, :] = lax.dot_general(
            row_bias[m].astype(jnp.bfloat16), top,
            (((0,), (0,)), ((), ())), preferred_element_type=jnp.float32,
        )

    pick = lambda a, b: jnp.where(end, a, b)
    order = [mate, pick(me_r, mir), pick(opp, me_r), pick(mir, opp)]

    def residual(k):
        m = order[k]
        scores = lax.dot_general(
            rows[...], cols[m], (((1,), (1,)), ((), ())), preferred_element_type=jnp.float32
        )
        weighted = weight[m] * (scores + shift[...] + col_bias[m, 0:1, :] - logs[m])
        wbuf[k] = weighted.astype(jnp.bfloat16)
        if k == 0:
            wrow[...] = weighted
        else:
            wrow[...] += weighted
        csum_out[m] = jnp.broadcast_to(jnp.sum(weighted, axis=0, keepdims=True), (EXTRA, side))

    def to_cols(k):
        col_out[order[k]] = lax.dot_general(
            wbuf[k], rows[...], (((0,), (0,)), ((), ())), preferred_element_type=jnp.float32
        ).astype(jnp.bfloat16)

    def send_col(k, when=None):
        m = order[k]
        send(col_out.at[m], col_in.at[me_r], co_send.at[m, 0], co_recv.at[me_r, 0], "row", m, when)

    def send_csum(k, when=None):
        m = order[k]
        send(csum_out.at[m], csum_in.at[me_r], cs_send.at[m], cs_recv.at[me_r], "row", m, when)

    def relay_e(pieces):
        for i in pieces:
            came(opp, i)
            outward[1][i].start()

    residual(0)
    to_cols(0)
    send_col(0, end)
    send_csum(0)
    @pl.when(inner)
    def _():
        bias_came(opp)
        bias_outward[1].start()
        relay_e((0, 1))


    residual(1)
    to_cols(1)
    send_csum(1, inner)
    pl.when(inner)(lambda: relay_e((2,)))

    @pl.when(end)
    def _():
        for i in range(PIECES):
            came(opp, i)
        bias_came(opp)

    residual(2)
    to_cols(2)
    send_csum(2, end)

    racc[...] = jnp.dot(
        jnp.concatenate([wbuf[0], wbuf[1]], axis=1),
        jnp.concatenate([cols[order[0]], cols[order[1]]], axis=0),
        preferred_element_type=jnp.float32,
    )

    @pl.when(inner)
    def _():
        relay_e((3,))

    send_col(0, inner)

    half = items // 2

    @pl.when(end)
    def _():
        bias_came(mir)
        for i in range(PIECES // 2):
            came(mir, i)
        first = jnp.concatenate([cols[mir, 0:half, :], jnp.zeros((half, width), jnp.bfloat16)], axis=0)
        scores = lax.dot_general(
            rows[...], first, (((1,), (1,)), ((), ())), preferred_element_type=jnp.float32
        )
        weighted = weight[mir] * (scores + shift[...] + col_bias[mir, 0:1, :] - logs[mir])
        col_out[mir, 0:half, :] = lax.dot_general(
            weighted.astype(jnp.bfloat16), rows[...], (((0,), (0,)), ((), ())), preferred_element_type=jnp.float32
        )[0:half].astype(jnp.bfloat16)
        for i in range(PIECES // 2):
            to_relay[1][i].start()
        for i in range(PIECES // 2, PIECES):
            came(mir, i)

    residual(3)
    columns = lax.dot_general(
        wbuf[3], rows[...], (((0,), (0,)), ((), ())), preferred_element_type=jnp.float32
    ).astype(jnp.bfloat16)
    col_out[order[3], half:items, :] = columns[half:items]

    @pl.when(end)
    def _():
        for i in range(PIECES // 2, PIECES):
            to_relay[1][i].start()

    @pl.when(inner)
    def _():
        col_out[opp, 0:half, :] = columns[0:half]


    @pl.when(end)
    def _():
        for copy in to_relay[0]:
            copy.start()

    send_csum(3)
    pair = jnp.concatenate([cols[order[2]], cols[order[3]]], axis=0)

    def row_terms(m):
        at = row_at(m)
        left = jnp.concatenate([wbuf[2, at, :], wbuf[3, at, :]], axis=1)
        return racc[at, :] + jnp.dot(left, pair, preferred_element_type=jnp.float32)

    def row_sums(m):
        return jnp.sum(jnp.transpose(wrow[row_at(m), :]), axis=0, keepdims=True)

    row_out[0] = row_terms(diag).astype(jnp.bfloat16)
    send(row_out.at[0], row_in.at[0], ro_send.at[0], ro_recv.at[0], "col", beside)
    row_out[1] = row_terms(beside).astype(jnp.bfloat16)
    send(row_out.at[1], row_in.at[1], ro_send.at[1], ro_recv.at[1], "col", beside)

    mine = row_terms(across)
    early = [(c, w) for c, w in sent if not any(c is d for d in to_relay[0] + to_relay[1] + from_relay[0] + from_relay[1])]
    landed(row_in.at[0], ro_recv.at[0], "col")
    row_out[2] = (mine + row_in[0].astype(jnp.float32)).astype(jnp.bfloat16)
    send(row_out.at[2], row_in.at[2], ro_send.at[2], ro_recv.at[2], "col", across)
    for m in (diag, across, beside):
        rsum_out[m] = jnp.broadcast_to(row_sums(m), (EXTRA, items))
        send(rsum_out.at[m], rsum_in.at[me_c], rs_send.at[m], rs_recv.at[me_c], "col", m)
    grad_ref[...] = row_terms(me_c) + col_out[me_r].astype(jnp.float32)
    btotal = row_sums(me_c) + csum_out[me_r, 0:1, :]
    late = [(c, w) for c, w in sent if not any(c is d for d, _ in early)]

    @pl.when(inner)
    def _():
        for k, m in ((1, opp), (0, mir)):
            for i in range(PIECES):
                landed(relay.at[k, part(i)], relay_recv.at[k, i], "row")
                col_out[m, part(i), :] = (
                    col_out[m, part(i), :].astype(jnp.float32) + relay[k, part(i), :].astype(jnp.float32)
                ).astype(jnp.bfloat16)
                from_relay[k][i].start()

    drain(early)
    landed(row_in.at[1], ro_recv.at[1], "col")
    landed(col_in.at[mate], co_recv.at[mate, 0], "row")
    grad_ref[...] += row_in[1].astype(jnp.float32) + col_in[mate].astype(jnp.float32)
    for m in (mate, opp, mir):
        landed(csum_in.at[m], cs_recv.at[m], "row")
        btotal += csum_in[m, 0:1, :]
    for m in (beside, across, diag):
        landed(rsum_in.at[m], rs_recv.at[m], "col")
        btotal += rsum_in[m, 0:1, :]
    gbias_ref[...] = btotal * 0.015625
    landed(row_in.at[2], ro_recv.at[2], "col")
    grad_ref[...] += row_in[2].astype(jnp.float32)

    last = pick(opp, mir)
    for i in range(PIECES):
        landed(col_in.at[last, part(i)], co_recv.at[last, i], "row")
        grad_ref[part(i), :] = (
            grad_ref[part(i), :] + col_in[last, part(i), :].astype(jnp.float32)
        ) * 0.0625
    drain(late)


def line_body(n_row, n_col, embedding, item_bias, counts, block_row, block_col, block_count):
    items, width = embedding.shape
    slots, side = counts.shape[2], counts.shape[3]
    span = n_col * items
    bf16, f32 = jnp.bfloat16, jnp.float32
    vmem = pl.BlockSpec(memory_space=pltpu.VMEM)
    hbm = pl.BlockSpec(memory_space=pltpu.HBM)
    dma = pltpu.SemaphoreType.DMA
    keep = lambda x: pltpu.with_memory_space_constraint(x, pltpu.HBM)
    grad, gbias = pl.pallas_call(
        line_kernel,
        out_shape=(
            jax.ShapeDtypeStruct((items, width), f32),
            jax.ShapeDtypeStruct((1, items), f32),
        ),
        in_specs=[hbm] * 6,
        out_specs=(vmem, vmem),
        scratch_shapes=[
            pltpu.SMEM((1, 1, slots), jnp.int32),
            pltpu.SMEM((1, 1, slots), jnp.int32),
            pltpu.SMEM((1, 1), jnp.int32),
            pltpu.VMEM((1, items), bf16),
            pltpu.VMEM((span, width), bf16),
            pltpu.VMEM((n_row, items, width), bf16),
            pltpu.VMEM((n_col, EXTRA, items), f32),
            pltpu.VMEM((n_row, EXTRA, items), f32),
            pltpu.VMEM((slots, side, side), jnp.int32),
            pltpu.VMEM((n_row, span, side), f32),
            pltpu.VMEM((n_row, span, side), f32),
            pltpu.VMEM((span, side), f32),
            pltpu.VMEM((span, side), f32),
            pltpu.VMEM((n_row, span, side), bf16),
            pltpu.VMEM((span, width), f32),
            pltpu.VMEM((n_row, items, width), bf16),
            pltpu.VMEM((n_row, items, width), bf16),
            pltpu.VMEM((2, items, width), bf16),
            pltpu.VMEM((3, items, width), bf16),
            pltpu.VMEM((3, items, width), bf16),
            pltpu.VMEM((n_row, EXTRA, items), f32),
            pltpu.VMEM((n_row, EXTRA, items), f32),
            pltpu.VMEM((n_col, EXTRA, items), f32),
            pltpu.VMEM((n_col, EXTRA, items), f32),
            dma((7,)),
            dma((2, PIECES)), dma((n_row, PIECES)), dma((n_row, PIECES)),
            dma((2,)), dma((n_row,)), dma((n_row,)),
            dma((PIECES + 1,)), dma((PIECES,)), dma((n_col, PIECES)),
            dma((2,)), dma((1,)), dma((n_col,)),
            dma((n_row, PIECES)), dma((n_row, PIECES)),
            dma((2, PIECES)), dma((2, PIECES)),
            dma((3,)), dma((3,)),
            dma((n_row,)), dma((n_row,)),
            dma((n_col,)), dma((n_col,)),
        ],
        compiler_params=pltpu.CompilerParams(
            collective_id=0, has_side_effects=True, vmem_limit_bytes=48 << 20
        ),
    )(
        keep(embedding), keep(item_bias.reshape(1, items)), keep(counts),
        keep(block_row), keep(block_col), block_count,
    )
    return grad, gbias.reshape(items)


def solution(mesh):
    placed = (
        P(("grp", "row", "col"), None),
        P(("grp", "row", "col")),
        P(("grp", "row"), "col", None, None, None),
        P(("grp", "row"), "col", None),
        P(("grp", "row"), "col", None),
        P(("grp", "row"), "col"),
    )

    def either(*args):
        n_row, n_col = mesh.shape["row"], mesh.shape["col"]
        line = n_row == 4 and n_col == 4 and args[0].shape[0] == args[2].shape[3]
        return (line_body if line else body)(n_row, n_col, *args)

    return jax.shard_map(
        either,
        mesh=mesh,
        in_specs=placed,
        out_specs=(P(("grp", "row", "col"), None), P(("grp", "row", "col"))),
        check_vma=False,
    )
```

```python
import functools

import jax
import jax.numpy as jnp
from jax import lax
from jax.experimental import pallas as pl
from jax.experimental.pallas import tpu as pltpu
from jax.sharding import PartitionSpec as P

MESH = pl.DeviceIdType.MESH
EXTRA = 8


def bias_rows(bias, width):
    items = bias.shape[1]
    first = lax.broadcasted_iota(jnp.int32, (EXTRA, items), 0) == 0
    rows = jnp.where(first, jnp.broadcast_to(bias, (EXTRA, items)), 0.0)
    if width > items:
        rows = jnp.concatenate([rows, jnp.zeros((EXTRA, width - items), jnp.float32)], axis=1)
    return rows.astype(jnp.bfloat16)


def nearest(me, k, n):
    inner = jnp.minimum(me, n - 1 - me)
    half = (k + 1) // 2
    both = me + half if k % 2 else me - half
    low = (me < n - 1 - me).astype(jnp.int32)
    one_side = low * k + (1 - low) * (n - 1 - k)
    return jnp.where(k <= 2 * inner, both, one_side)


def kernel(
    n_row, n_col, emb_ref, bias_hbm, counts_ref, brow_hbm, bcol_hbm, bcount_hbm,
    grad_ref, gbias_ref,
    brow_ref, bcol_ref, bcount_ref, bias_ref, rows, cols, tally, weight, logs, shift, wrow, racc, row_out, col_out, row_in, col_in, col_own,
    local_sem, rs_send, rs_recv, cs_send, cs_recv, ro_send, ro_recv, co_send, co_recv,
    rs_pass, cs_pass, last_w,
):
    items, width = emb_ref.shape
    slots, side = counts_ref.shape[2], counts_ref.shape[3]
    me_r, me_c = lax.axis_index("row"), lax.axis_index("col")
    span = n_col * items
    n_rb = span // side
    n_cb = n_row * items // side
    group = side // items

    load_bias = pltpu.make_async_copy(bias_hbm, bias_ref, local_sem.at[3])
    load_bias.start()
    load_emb = pltpu.make_async_copy(emb_ref, cols.at[me_r, pl.ds(0, items)], local_sem.at[0])
    load_emb.start()
    load_own = pltpu.make_async_copy(emb_ref, rows.at[me_c, pl.ds(0, items)], local_sem.at[1])
    load_own.start()
    loads = [
        pltpu.make_async_copy(src, dst, local_sem.at[4 + i])
        for i, (src, dst) in enumerate(
            ((brow_hbm, brow_ref), (bcol_hbm, bcol_ref), (bcount_hbm, bcount_ref))
        )
    ]
    for load in loads:
        load.start()
    load_counts = pltpu.make_async_copy(counts_ref.at[0, 0], tally, local_sem.at[2])
    load_counts.start()

    barrier = pltpu.get_barrier_semaphore()
    has_up, has_down = me_r < n_row - 1, me_r > 0
    chips = n_col // 2
    core, chip = lax.rem(me_c, 2), me_c // 2
    beside = me_c + 1 - 2 * core
    away = [lax.rem(chip + k, chips) * 2 + core for k in range(1, chips)]

    def greet(axis, to):
        pl.semaphore_signal(barrier, inc=1, device_id={axis: to}, device_id_type=MESH)

    pl.when(has_up)(lambda: greet("row", me_r + 1))
    pl.when(has_down)(lambda: greet("row", me_r - 1))
    for to in away + [beside]:
        greet("col", to)
    load_bias.wait()
    packed = bias_rows(bias_ref[...].astype(jnp.float32), width)
    cols[me_r, items : items + EXTRA, :] = packed
    rows[me_c, items : items + EXTRA, :] = packed
    load_counts.wait()
    for load in loads:
        load.wait()
    listed = bcount_ref[0, 0]

    def position(p, carry):
        bi, bj = p // n_cb, lax.rem(p, n_cb)
        slot = jnp.int32(0)
        found = jnp.int32(0)
        for s in range(slots):
            hit = jnp.logical_and(
                jnp.logical_and(brow_ref[0, 0, s] == bi, bcol_ref[0, 0, s] == bj), s < listed
            )
            slot = jnp.where(hit, s, slot)
            found = jnp.where(hit, 1, found)
        x = tally[slot] * found
        logged = jnp.log(jnp.maximum(x.astype(jnp.float32), 1.0))
        w = jnp.where(
            x > 0, jnp.minimum(1.0, jnp.exp(0.75 * (logged - jnp.log(jnp.float32(100.0))))), 0.0
        )
        at = pl.ds(pl.multiple_of(bi * side, side), side)
        weight[bj, at, :] = w
        logs[bj, at, :] = logged
        return carry


    load_emb.wait()
    load_own.wait()
    beyond = has_up.astype(jnp.int32) + has_down.astype(jnp.int32)
    pl.semaphore_wait(barrier, beyond + len(away) + 1)

    sent = []

    def send(src, dst, send_sem, recv_sem, axis, to, when=None):
        copy = pltpu.make_async_remote_copy(
            src_ref=src, dst_ref=dst, send_sem=send_sem, recv_sem=recv_sem,
            device_id={axis: to}, device_id_type=MESH,
        )
        if when is None:
            copy.start()
        else:
            pl.when(when)(copy.start)
        sent.append((copy, when))

    halves = (pl.ds(0, items // 2), pl.ds(items // 2, items - items // 2 + EXTRA))
    for h in range(2):
        mine = cols.at[me_r, halves[h]]
        send(mine, mine, cs_send.at[0, h], cs_recv.at[me_r, h], "row", me_r + 1, has_up)
        send(mine, mine, cs_send.at[1, h], cs_recv.at[me_r, h], "row", me_r - 1, has_down)
    mine = rows.at[me_c]
    for to in away:
        send(mine, mine, rs_send.at[to], rs_recv.at[me_c], "col", to)
    send(mine, mine, rs_send.at[beside], rs_recv.at[me_c], "col", beside)
    lax.fori_loop(0, n_rb * n_cb, position, 0)

    def arrived(buf, sem, axis, slot):
        pltpu.make_async_remote_copy(
            src_ref=buf.at[slot], dst_ref=buf.at[slot], send_sem=sem.at[slot],
            recv_sem=sem.at[slot], device_id={axis: slot}, device_id_type=MESH,
        ).wait_recv()

    def take(ms, when=None):
        for h in range(2):
            for m in ms:
                piece = cols.at[m, halves[h]]
                landed = pltpu.make_async_remote_copy(
                    src_ref=piece, dst_ref=piece, send_sem=cs_pass.at[m, h],
                    recv_sem=cs_recv.at[m, h], device_id={"row": m}, device_id_type=MESH,
                )
                if when is None:
                    landed.wait_recv()
                else:
                    pl.when(when)(landed.wait_recv)
                to = me_r + 2 * (m < me_r).astype(jnp.int32) - 1
                ok = jnp.logical_and(to >= 0, to < n_row)
                if when is not None:
                    ok = jnp.logical_and(ok, when)
                send(piece, piece, cs_pass.at[m, h], cs_recv.at[m, h], "row", to, ok)

    early = 2 if group == 1 and n_cb == 4 else 0
    inner = jnp.logical_and(has_up, has_down)
    if early:
        take([nearest(me_r, k, n_row) for k in range(1, early + 1)])
    for m in away:
        arrived(rows, rs_recv, "col", m)
        send(rows.at[m], rows.at[m], rs_pass.at[m], rs_recv.at[m], "col", beside)
    arrived(rows, rs_recv, "col", beside)
    for m in away:
        arrived(rows, rs_recv, "col", m + 1 - 2 * core)
    top = (lax.broadcasted_iota(jnp.int32, (EXTRA, side), 0) == 0).astype(jnp.float32).astype(jnp.bfloat16)
    for i in range(n_col):
        shift[i * items : (i + 1) * items, :] = lax.dot_general(
            rows[i, items : items + EXTRA, 0:items], top,
            (((0,), (0,)), ((), ())), preferred_element_type=jnp.float32,
        )

    all_rows = jnp.concatenate([rows[i, 0:items, :] for i in range(n_col)], axis=0)
    me_g = me_r // group
    for k in range(n_cb):
        jb = nearest(me_g, k, n_cb)
        if k == 0:
            members = [me_g * group + lax.rem(me_r + t, group) for t in range(1, group)]
        else:
            members = [jb * group + t for t in range(group)]
        if early and k == 1:
            take([nearest(me_r, early + 1, n_row)], inner)
        elif early and k == early + 1:
            take(members, jnp.logical_not(inner))
        elif not early:
            take(members)
        block = jnp.concatenate([cols[jb * group + t, 0:items, :] for t in range(group)], axis=0)
        cshift = jnp.concatenate(
            [cols[jb * group + t, items : items + EXTRA, 0:items].astype(jnp.float32)[0:1] for t in range(group)],
            axis=1,
        )
        scores = lax.dot_general(
            all_rows, block, (((1,), (1,)), ((), ())), preferred_element_type=jnp.float32
        )
        weighted = weight[jb] * (scores + shift[...] + cshift - logs[jb])
        rounded = weighted.astype(jnp.bfloat16)
        to_cols = lax.dot_general(
            rounded, all_rows, (((0,), (0,)), ((), ())), preferred_element_type=jnp.float32
        )
        sums = jnp.sum(weighted, axis=0, keepdims=True)
        if k == 0:
            wrow[...] = weighted
        else:
            wrow[...] += weighted
        for t in range(group):
            to = jb * group + t
            part = to_cols[t * items : (t + 1) * items]
            part_sums = sums[:, t * items : (t + 1) * items]
            col_out[to, 0:items, :] = part.astype(jnp.bfloat16)
            col_out[to, items : items + EXTRA, :] = bias_rows(part_sums, width)
            if k == 0:
                if group == 1:
                    col_own[0:items, :] = part
                    col_own[items : items + 1, 0:items] = part_sums
                else:

                    @pl.when(to == me_r)
                    def _():
                        col_own[0:items, :] = part
                        col_own[items : items + 1, 0:items] = part_sums
        for m in members:
            send(col_out.at[m], col_in.at[me_r], co_send.at[m], co_recv.at[me_r], "row", m)
        if k == n_cb - 1:
            last_w[...] = rounded
            last_block = block
        else:
            to_rows = jnp.dot(rounded, block, preferred_element_type=jnp.float32)
            if k == 0:
                racc[...] = to_rows
            else:
                racc[...] += to_rows

    def row_terms(at):
        return racc[at, :] + jnp.dot(
            last_w[at, :], last_block, preferred_element_type=jnp.float32
        )

    def row_sums(i):
        at = pl.ds(pl.multiple_of(i * items, items), items)
        return jnp.sum(jnp.transpose(wrow[at, :]), axis=0, keepdims=True)

    across = [a + t * (1 - 2 * core) for a in away for t in (0, 1)]
    for to in across + [beside]:
        at = pl.ds(pl.multiple_of(to * items, items), items)
        row_out[to, 0:items, :] = row_terms(at).astype(jnp.bfloat16)
        row_out[to, items : items + EXTRA, :] = bias_rows(row_sums(to), width)
        send(row_out.at[to], row_in.at[me_c], ro_send.at[to], ro_recv.at[me_c], "col", to)

    at = pl.ds(pl.multiple_of(me_c * items, items), items)
    total = row_terms(at) + col_own[0:items, :]
    btotal = row_sums(me_c) + col_own[items : items + 1, 0:items]

    def added(total, btotal, buf, slot):
        return (
            total + buf[slot, 0:items, :].astype(jnp.float32),
            btotal + buf[slot, items : items + EXTRA, 0:items].astype(jnp.float32)[0:1],
        )

    for k in range(1, n_col):
        slot = lax.rem(me_c + n_col - k, n_col)
        arrived(row_in, ro_recv, "col", slot)
        total, btotal = added(total, btotal, row_in, slot)
    for k in range(1, n_row):
        slot = nearest(me_r, k, n_row)
        arrived(col_in, co_recv, "row", slot)
        total, btotal = added(total, btotal, col_in, slot)
    grad_ref[...] = total * 0.0625
    gbias_ref[...] = btotal * 0.015625
    for copy, when in sent:
        if when is None:
            copy.wait_send()
        else:
            pl.when(when)(copy.wait_send)


def body(n_row, n_col, embedding, item_bias, counts, block_row, block_col, block_count):
    items, width = embedding.shape
    slots, side = counts.shape[2], counts.shape[3]
    span, across = n_col * items, n_row * items // side
    vmem = pl.BlockSpec(memory_space=pltpu.VMEM)
    smem = pl.BlockSpec(memory_space=pltpu.SMEM)
    hbm = pl.BlockSpec(memory_space=pltpu.HBM)
    tall = items + EXTRA
    dma = pltpu.SemaphoreType.DMA
    keep = lambda x: pltpu.with_memory_space_constraint(x, pltpu.HBM)
    grad, gbias = pl.pallas_call(
        functools.partial(kernel, n_row, n_col),
        out_shape=(
            jax.ShapeDtypeStruct((items, width), jnp.float32),
            jax.ShapeDtypeStruct((1, items), jnp.float32),
        ),
        in_specs=[hbm] * 6,
        out_specs=(vmem, vmem),
        scratch_shapes=[
            pltpu.SMEM((1, 1, slots), jnp.int32),
            pltpu.SMEM((1, 1, slots), jnp.int32),
            pltpu.SMEM((1, 1), jnp.int32),
            pltpu.VMEM((1, items), jnp.bfloat16),
            pltpu.VMEM((n_col, tall, width), jnp.bfloat16),
            pltpu.VMEM((n_row, tall, width), jnp.bfloat16),
            pltpu.VMEM((slots, side, side), jnp.int32),
            pltpu.VMEM((across, span, side), jnp.float32),
            pltpu.VMEM((across, span, side), jnp.float32),
            pltpu.VMEM((span, side), jnp.float32),
            pltpu.VMEM((span, side), jnp.float32),
            pltpu.VMEM((span, width), jnp.float32),
            pltpu.VMEM((n_col, tall, width), jnp.bfloat16),
            pltpu.VMEM((n_row, tall, width), jnp.bfloat16),
            pltpu.VMEM((n_col, tall, width), jnp.bfloat16),
            pltpu.VMEM((n_row, tall, width), jnp.bfloat16),
            pltpu.VMEM((items + 8, width), jnp.float32),
            dma((7,)),
            dma((n_col,)), dma((n_col,)),
            dma((2, 2)), dma((n_row, 2)),
            dma((n_col,)), dma((n_col,)),
            dma((n_row,)), dma((n_row,)),
            dma((n_col,)), dma((n_row, 2)),
            pltpu.VMEM((span, side), jnp.bfloat16),
        ],
        compiler_params=pltpu.CompilerParams(
            collective_id=0, has_side_effects=True, vmem_limit_bytes=48 << 20
        ),
    )(
        keep(embedding), keep(item_bias.reshape(1, items)), keep(counts),
        block_row, block_col, block_count,
    )
    return grad, gbias.reshape(items)


PIECES = 4


def line_kernel(
    emb_hbm, bias_hbm, counts_hbm, brow_hbm, bcol_hbm, bcount_hbm,
    grad_ref, gbias_ref,
    brow_ref, bcol_ref, bcount_ref, bias_ref, rows, cols, row_bias, col_bias, tally, weight, logs, shift, wrow, wbuf, racc,
    col_out, col_in, relay, row_out, row_in, csum_out, csum_in, rsum_out, rsum_in,
    load_sem, e_send, e_pass, e_recv, eb_send, eb_pass, eb_recv, r_send, r_pass, r_recv, rb_send, rb_pass, rb_recv,
    co_send, co_recv, relay_send, relay_recv, ro_send, ro_recv, cs_send, cs_recv, rs_send, rs_recv,
):
    items, width = emb_hbm.shape
    slots, side = counts_hbm.shape[2], counts_hbm.shape[3]
    n_row, n_col = cols.shape[0], rows.shape[0] // items
    piece = items // PIECES
    me_r, me_c = lax.axis_index("row"), lax.axis_index("col")
    mate, opp, mir = me_r + 1 - 2 * lax.rem(me_r, 2), lax.rem(me_r + 2, n_row), n_row - 1 - me_r
    end = jnp.logical_or(me_r == 0, me_r == n_row - 1)
    inner = jnp.logical_not(end)
    core = lax.rem(me_c, 2)
    beside, across = me_c + 1 - 2 * core, lax.rem(me_c + 2, n_col)
    diag = across + 1 - 2 * core

    def part(i):
        return pl.ds(i * piece, piece)

    def row_at(m, i=0, height=items):
        return pl.ds(pl.multiple_of(m * items + i * piece, piece), height)

    load_bias = pltpu.make_async_copy(bias_hbm, bias_ref, load_sem.at[0])
    load_emb = pltpu.make_async_copy(emb_hbm, cols.at[me_r], load_sem.at[1])
    load_own = pltpu.make_async_copy(emb_hbm, rows.at[row_at(me_c)], load_sem.at[2])
    load_lists = [
        pltpu.make_async_copy(src, dst, load_sem.at[3 + i])
        for i, (src, dst) in enumerate(((brow_hbm, brow_ref), (bcol_hbm, bcol_ref), (bcount_hbm, bcount_ref)))
    ]
    load_counts = pltpu.make_async_copy(counts_hbm.at[0, 0], tally, load_sem.at[6])
    for load in [load_emb, load_own, load_bias] + load_lists + [load_counts]:
        load.start()

    barrier = pltpu.get_barrier_semaphore()

    def greet(axis, to):
        pl.semaphore_signal(barrier, inc=1, device_id={axis: to}, device_id_type=MESH)

    greet("row", mate)
    pl.when(inner)(lambda: greet("row", mir))
    greet("col", across)
    greet("col", beside)

    load_bias.wait()
    own_bias = jnp.broadcast_to(bias_ref[...].astype(jnp.float32), (EXTRA, items))
    row_bias[me_c] = own_bias
    col_bias[me_r] = own_bias
    load_emb.wait()
    load_own.wait()
    pl.semaphore_wait(barrier, 3 + inner.astype(jnp.int32))

    sent = []

    def remote(src, dst, send_sem, recv_sem, axis, to):
        return pltpu.make_async_remote_copy(
            src_ref=src, dst_ref=dst, send_sem=send_sem, recv_sem=recv_sem,
            device_id={axis: to}, device_id_type=MESH,
        )

    def send(src, dst, send_sem, recv_sem, axis, to, when=None):
        copy = remote(src, dst, send_sem, recv_sem, axis, to)
        if when is None:
            copy.start()
        else:
            pl.when(when)(copy.start)
        sent.append((copy, when))

    def landed(dst, recv_sem, axis):
        remote(dst, dst, recv_sem, recv_sem, axis, me_r if axis == "row" else me_c).wait_recv()

    def drain(copies):
        for group, when in ((None, None), (end, end), (inner, inner)):
            these = [copy for copy, w in copies if w is group]
            if when is None:
                for copy in these:
                    copy.wait_send()
            elif these:

                @pl.when(when)
                def _():
                    for copy in these:
                        copy.wait_send()

    own = col_bias.at[me_r]
    send(own, own, eb_send.at[0], eb_recv.at[me_r], "row", mate)
    send(own, own, eb_send.at[1], eb_recv.at[me_r], "row", mir, inner)
    own = row_bias.at[me_c]
    send(own, own, rb_send.at[0], rb_recv.at[me_c], "col", across)
    send(own, own, rb_send.at[1], rb_recv.at[me_c], "col", beside)

    for i in range(PIECES):
        own = cols.at[me_r, part(i)]
        send(own, own, e_send.at[0, i], e_recv.at[me_r, i], "row", mate)
        send(own, own, e_send.at[1, i], e_recv.at[me_r, i], "row", mir, inner)
        own = rows.at[row_at(me_c, i, piece)]
        send(own, own, r_send.at[i], r_recv.at[me_c, i], "col", across)
    own = rows.at[row_at(me_c)]
    send(own, own, r_send.at[PIECES], r_recv.at[me_c, 0], "col", beside)

    for load in load_lists + [load_counts]:
        load.wait()
    listed = bcount_ref[0, 0]
    code = [
        jnp.where(s < listed, brow_ref[0, 0, s] * n_row + bcol_ref[0, 0, s], -1) for s in range(slots)
    ]

    def position(p, carry):
        bi, bj = p // n_row, lax.rem(p, n_row)
        slot = jnp.int32(0)
        found = jnp.int32(0)
        for s in range(slots):
            hit = code[s] == p
            slot = jnp.where(hit, s, slot)
            found = jnp.where(hit, 1, found)
        x = tally[slot] * found
        logged = jnp.log(jnp.maximum(x.astype(jnp.float32), 1.0))
        w = jnp.where(
            x > 0, jnp.minimum(1.0, jnp.exp(0.75 * (logged - jnp.log(jnp.float32(100.0))))), 0.0
        )
        at = pl.ds(pl.multiple_of(bi * side, side), side)
        weight[bj, at, :] = w
        logs[bj, at, :] = logged
        return carry

    lax.fori_loop(0, n_col * n_row, position, 0)

    def came(m, i):
        landed(cols.at[m, part(i)], e_recv.at[m, i], "row")

    def hand(m, i, to):
        return remote(
            cols.at[m, part(i)], cols.at[m, part(i)], e_pass.at[m, i], e_recv.at[m, i], "row", to
        )

    def bias_came(m):
        landed(col_bias.at[m], eb_recv.at[m], "row")

    def bias_hand(m, to):
        return remote(col_bias.at[m], col_bias.at[m], eb_pass.at[m], eb_recv.at[m], "row", to)

    def later(copy, when):
        sent.append((copy, when))
        return copy

    outward = [[later(hand(m, i, mate), inner) for i in range(PIECES)] for m in (mir, opp)]
    inward = [later(hand(mate, i, mir), inner) for i in range(PIECES)]
    bias_outward = [later(bias_hand(m, mate), inner) for m in (mir, opp)]
    bias_inward = later(bias_hand(mate, mir), inner)
    to_relay = [
        [
            later(remote(col_out.at[m, part(i)], relay.at[k, part(i)], relay_send.at[k, i], relay_recv.at[k, i], "row", mate), end)
            for i in range(PIECES)
        ]
        for k, m in enumerate((opp, mir))
    ]
    from_relay = [
        [
            later(remote(col_out.at[m, part(i)], col_in.at[me_r, part(i)], co_send.at[m, i], co_recv.at[me_r, i], "row", m), inner)
            for i in range(PIECES)
        ]
        for m in (mir, opp)
    ]

    for i in range(PIECES):
        came(mate, i)
        if i == 0:
            bias_came(mate)

        @pl.when(inner)
        def _():
            if i == 0:
                bias_inward.start()
            inward[i].start()
            came(mir, i)
            if i == 0:
                bias_came(mir)
                bias_outward[0].start()
            outward[0][i].start()

        if i == 0:
            landed(row_bias.at[across], rb_recv.at[across], "col")
            send(row_bias.at[across], row_bias.at[across], rb_pass.at[0], rb_recv.at[across], "col", beside)
        landed(rows.at[row_at(across, i, piece)], r_recv.at[across, i], "col")
        passed = rows.at[row_at(across, i, piece)]
        send(passed, passed, r_pass.at[i], r_recv.at[across, i], "col", beside)

    landed(rows.at[row_at(beside)], r_recv.at[beside, 0], "col")
    landed(row_bias.at[beside], rb_recv.at[beside], "col")
    for i in range(PIECES):
        landed(rows.at[row_at(diag, i, piece)], r_recv.at[diag, i], "col")
    landed(row_bias.at[diag], rb_recv.at[diag], "col")

    top = (lax.broadcasted_iota(jnp.int32, (EXTRA, side), 0) == 0).astype(jnp.float32).astype(jnp.bfloat16)
    for m in range(n_col):
        shift[m * items : (m + 1) * items, :] = lax.dot_general(
            row_bias[m].astype(jnp.bfloat16), top,
            (((0,), (0,)), ((), ())), preferred_element_type=jnp.float32,
        )

    pick = lambda a, b: jnp.where(end, a, b)
    order = [mate, pick(me_r, mir), pick(opp, me_r), pick(mir, opp)]

    def residual(k):
        m = order[k]
        scores = lax.dot_general(
            rows[...], cols[m], (((1,), (1,)), ((), ())), preferred_element_type=jnp.float32
        )
        weighted = weight[m] * (scores + shift[...] + col_bias[m, 0:1, :] - logs[m])
        wbuf[k] = weighted.astype(jnp.bfloat16)
        if k == 0:
            wrow[...] = weighted
        else:
            wrow[...] += weighted
        csum_out[m] = jnp.broadcast_to(jnp.sum(weighted, axis=0, keepdims=True), (EXTRA, side))

    def to_cols(k):
        col_out[order[k]] = lax.dot_general(
            wbuf[k], rows[...], (((0,), (0,)), ((), ())), preferred_element_type=jnp.float32
        ).astype(jnp.bfloat16)

    def send_col(k, when=None):
        m = order[k]
        send(col_out.at[m], col_in.at[me_r], co_send.at[m, 0], co_recv.at[me_r, 0], "row", m, when)

    def send_csum(k, when=None):
        m = order[k]
        send(csum_out.at[m], csum_in.at[me_r], cs_send.at[m], cs_recv.at[me_r], "row", m, when)

    def relay_e(pieces):
        for i in pieces:
            came(opp, i)
            outward[1][i].start()

    residual(0)
    to_cols(0)
    send_col(0, end)
    send_csum(0)
    @pl.when(inner)
    def _():
        bias_came(opp)
        bias_outward[1].start()
        relay_e((0, 1))


    residual(1)
    to_cols(1)
    send_csum(1, inner)
    pl.when(inner)(lambda: relay_e((2,)))

    @pl.when(end)
    def _():
        for i in range(PIECES):
            came(opp, i)
        bias_came(opp)

    residual(2)
    to_cols(2)
    send_csum(2, end)

    racc[...] = jnp.dot(
        jnp.concatenate([wbuf[0], wbuf[1]], axis=1),
        jnp.concatenate([cols[order[0]], cols[order[1]]], axis=0),
        preferred_element_type=jnp.float32,
    )

    @pl.when(inner)
    def _():
        relay_e((3,))

    send_col(0, inner)

    groups = ((0, 2), (2, 3))
    begun = groups[-1][1]

    @pl.when(end)
    def _():
        bias_came(mir)
        for a, b in groups:
            for i in range(a, b):
                came(mir, i)
            some = [jnp.zeros((n * piece, width), jnp.bfloat16) for n in (a, PIECES - b)]
            some = [some[0]] * (a > 0) + [cols[mir, a * piece : b * piece, :]] + [some[1]] * (b < PIECES)
            scores = lax.dot_general(
                rows[...], jnp.concatenate(some, axis=0), (((1,), (1,)), ((), ())), preferred_element_type=jnp.float32
            )
            weighted = weight[mir] * (scores + shift[...] + col_bias[mir, 0:1, :] - logs[mir])
            col_out[mir, a * piece : b * piece, :] = lax.dot_general(
                weighted.astype(jnp.bfloat16), rows[...], (((0,), (0,)), ((), ())), preferred_element_type=jnp.float32
            )[a * piece : b * piece].astype(jnp.bfloat16)
            for i in range(a, b):
                to_relay[1][i].start()
        for i in range(begun, PIECES):
            came(mir, i)

    residual(3)
    columns = lax.dot_general(
        wbuf[3], rows[...], (((0,), (0,)), ((), ())), preferred_element_type=jnp.float32
    ).astype(jnp.bfloat16)
    col_out[order[3], begun * piece :, :] = columns[begun * piece :]

    @pl.when(end)
    def _():
        for i in range(begun, PIECES):
            to_relay[1][i].start()

    @pl.when(inner)
    def _():
        col_out[opp, : begun * piece, :] = columns[: begun * piece]


    @pl.when(end)
    def _():
        for copy in to_relay[0]:
            copy.start()

    send_csum(3)
    pair = jnp.concatenate([cols[order[2]], cols[order[3]]], axis=0)

    def row_terms(m):
        at = row_at(m)
        left = jnp.concatenate([wbuf[2, at, :], wbuf[3, at, :]], axis=1)
        return racc[at, :] + jnp.dot(left, pair, preferred_element_type=jnp.float32)

    def row_sums(m):
        return jnp.sum(jnp.transpose(wrow[row_at(m), :]), axis=0, keepdims=True)

    row_out[0] = row_terms(diag).astype(jnp.bfloat16)
    send(row_out.at[0], row_in.at[0], ro_send.at[0], ro_recv.at[0], "col", beside)
    row_out[1] = row_terms(beside).astype(jnp.bfloat16)
    send(row_out.at[1], row_in.at[1], ro_send.at[1], ro_recv.at[1], "col", beside)

    mine = row_terms(across)
    early = [(c, w) for c, w in sent if not any(c is d for d in to_relay[0] + to_relay[1] + from_relay[0] + from_relay[1])]
    landed(row_in.at[0], ro_recv.at[0], "col")
    row_out[2] = (mine + row_in[0].astype(jnp.float32)).astype(jnp.bfloat16)
    send(row_out.at[2], row_in.at[2], ro_send.at[2], ro_recv.at[2], "col", across)
    for m in (diag, across, beside):
        rsum_out[m] = jnp.broadcast_to(row_sums(m), (EXTRA, items))
        send(rsum_out.at[m], rsum_in.at[me_c], rs_send.at[m], rs_recv.at[me_c], "col", m)
    grad_ref[...] = row_terms(me_c) + col_out[me_r].astype(jnp.float32)
    btotal = row_sums(me_c) + csum_out[me_r, 0:1, :]
    late = [(c, w) for c, w in sent if not any(c is d for d, _ in early)]

    @pl.when(inner)
    def _():
        for k, m in ((1, opp), (0, mir)):
            for i in range(PIECES):
                landed(relay.at[k, part(i)], relay_recv.at[k, i], "row")
                col_out[m, part(i), :] = (
                    col_out[m, part(i), :].astype(jnp.float32) + relay[k, part(i), :].astype(jnp.float32)
                ).astype(jnp.bfloat16)
                from_relay[k][i].start()

    drain(early)
    landed(row_in.at[1], ro_recv.at[1], "col")
    landed(col_in.at[mate], co_recv.at[mate, 0], "row")
    grad_ref[...] += row_in[1].astype(jnp.float32) + col_in[mate].astype(jnp.float32)
    for m in (mate, opp, mir):
        landed(csum_in.at[m], cs_recv.at[m], "row")
        btotal += csum_in[m, 0:1, :]
    for m in (beside, across, diag):
        landed(rsum_in.at[m], rs_recv.at[m], "col")
        btotal += rsum_in[m, 0:1, :]
    gbias_ref[...] = btotal * 0.015625
    landed(row_in.at[2], ro_recv.at[2], "col")
    grad_ref[...] += row_in[2].astype(jnp.float32)

    last = pick(opp, mir)
    for i in range(PIECES):
        landed(col_in.at[last, part(i)], co_recv.at[last, i], "row")
        grad_ref[part(i), :] = (
            grad_ref[part(i), :] + col_in[last, part(i), :].astype(jnp.float32)
        ) * 0.0625
    drain(late)


def line_body(n_row, n_col, embedding, item_bias, counts, block_row, block_col, block_count):
    items, width = embedding.shape
    slots, side = counts.shape[2], counts.shape[3]
    span = n_col * items
    bf16, f32 = jnp.bfloat16, jnp.float32
    vmem = pl.BlockSpec(memory_space=pltpu.VMEM)
    hbm = pl.BlockSpec(memory_space=pltpu.HBM)
    dma = pltpu.SemaphoreType.DMA
    keep = lambda x: pltpu.with_memory_space_constraint(x, pltpu.HBM)
    grad, gbias = pl.pallas_call(
        line_kernel,
        out_shape=(
            jax.ShapeDtypeStruct((items, width), f32),
            jax.ShapeDtypeStruct((1, items), f32),
        ),
        in_specs=[hbm] * 6,
        out_specs=(vmem, vmem),
        scratch_shapes=[
            pltpu.SMEM((1, 1, slots), jnp.int32),
            pltpu.SMEM((1, 1, slots), jnp.int32),
            pltpu.SMEM((1, 1), jnp.int32),
            pltpu.VMEM((1, items), bf16),
            pltpu.VMEM((span, width), bf16),
            pltpu.VMEM((n_row, items, width), bf16),
            pltpu.VMEM((n_col, EXTRA, items), f32),
            pltpu.VMEM((n_row, EXTRA, items), f32),
            pltpu.VMEM((slots, side, side), jnp.int32),
            pltpu.VMEM((n_row, span, side), f32),
            pltpu.VMEM((n_row, span, side), f32),
            pltpu.VMEM((span, side), f32),
            pltpu.VMEM((span, side), f32),
            pltpu.VMEM((n_row, span, side), bf16),
            pltpu.VMEM((span, width), f32),
            pltpu.VMEM((n_row, items, width), bf16),
            pltpu.VMEM((n_row, items, width), bf16),
            pltpu.VMEM((2, items, width), bf16),
            pltpu.VMEM((3, items, width), bf16),
            pltpu.VMEM((3, items, width), bf16),
            pltpu.VMEM((n_row, EXTRA, items), f32),
            pltpu.VMEM((n_row, EXTRA, items), f32),
            pltpu.VMEM((n_col, EXTRA, items), f32),
            pltpu.VMEM((n_col, EXTRA, items), f32),
            dma((7,)),
            dma((2, PIECES)), dma((n_row, PIECES)), dma((n_row, PIECES)),
            dma((2,)), dma((n_row,)), dma((n_row,)),
            dma((PIECES + 1,)), dma((PIECES,)), dma((n_col, PIECES)),
            dma((2,)), dma((1,)), dma((n_col,)),
            dma((n_row, PIECES)), dma((n_row, PIECES)),
            dma((2, PIECES)), dma((2, PIECES)),
            dma((3,)), dma((3,)),
            dma((n_row,)), dma((n_row,)),
            dma((n_col,)), dma((n_col,)),
        ],
        compiler_params=pltpu.CompilerParams(
            collective_id=0, has_side_effects=True, vmem_limit_bytes=48 << 20
        ),
    )(
        keep(embedding), keep(item_bias.reshape(1, items)), keep(counts),
        keep(block_row), keep(block_col), block_count,
    )
    return grad, gbias.reshape(items)


def solution(mesh):
    placed = (
        P(("grp", "row", "col"), None),
        P(("grp", "row", "col")),
        P(("grp", "row"), "col", None, None, None),
        P(("grp", "row"), "col", None),
        P(("grp", "row"), "col", None),
        P(("grp", "row"), "col"),
    )

    def either(*args):
        n_row, n_col = mesh.shape["row"], mesh.shape["col"]
        line = n_row == 4 and n_col == 4 and args[0].shape[0] == args[2].shape[3]
        return (line_body if line else body)(n_row, n_col, *args)

    return jax.shard_map(
        either,
        mesh=mesh,
        in_specs=placed,
        out_specs=(P(("grp", "row", "col"), None), P(("grp", "row", "col"))),
        check_vma=False,
    )
```

```python
import functools

import jax
import jax.numpy as jnp
from jax import lax
from jax.experimental import pallas as pl
from jax.experimental.pallas import tpu as pltpu
from jax.sharding import PartitionSpec as P

MESH = pl.DeviceIdType.MESH
EXTRA = 8


def bias_rows(bias, width):
    items = bias.shape[1]
    first = lax.broadcasted_iota(jnp.int32, (EXTRA, items), 0) == 0
    rows = jnp.where(first, jnp.broadcast_to(bias, (EXTRA, items)), 0.0)
    if width > items:
        rows = jnp.concatenate([rows, jnp.zeros((EXTRA, width - items), jnp.float32)], axis=1)
    return rows.astype(jnp.bfloat16)


def nearest(me, k, n):
    inner = jnp.minimum(me, n - 1 - me)
    half = (k + 1) // 2
    both = me + half if k % 2 else me - half
    low = (me < n - 1 - me).astype(jnp.int32)
    one_side = low * k + (1 - low) * (n - 1 - k)
    return jnp.where(k <= 2 * inner, both, one_side)


def kernel(
    n_row, n_col, emb_ref, bias_hbm, counts_ref, brow_hbm, bcol_hbm, bcount_hbm,
    grad_ref, gbias_ref,
    brow_ref, bcol_ref, bcount_ref, bias_ref, rows, cols, tally, weight, logs, shift, wrow, racc, row_out, col_out, row_in, col_in, col_own,
    local_sem, rs_send, rs_recv, cs_send, cs_recv, ro_send, ro_recv, co_send, co_recv,
    rs_pass, cs_pass, last_w,
):
    items, width = emb_ref.shape
    slots, side = counts_ref.shape[2], counts_ref.shape[3]
    me_r, me_c = lax.axis_index("row"), lax.axis_index("col")
    span = n_col * items
    n_rb = span // side
    n_cb = n_row * items // side
    group = side // items

    load_bias = pltpu.make_async_copy(bias_hbm, bias_ref, local_sem.at[3])
    load_bias.start()
    load_emb = pltpu.make_async_copy(emb_ref, cols.at[me_r, pl.ds(0, items)], local_sem.at[0])
    load_emb.start()
    load_own = pltpu.make_async_copy(emb_ref, rows.at[me_c, pl.ds(0, items)], local_sem.at[1])
    load_own.start()
    loads = [
        pltpu.make_async_copy(src, dst, local_sem.at[4 + i])
        for i, (src, dst) in enumerate(
            ((brow_hbm, brow_ref), (bcol_hbm, bcol_ref), (bcount_hbm, bcount_ref))
        )
    ]
    for load in loads:
        load.start()
    load_counts = pltpu.make_async_copy(counts_ref.at[0, 0], tally, local_sem.at[2])
    load_counts.start()

    barrier = pltpu.get_barrier_semaphore()
    has_up, has_down = me_r < n_row - 1, me_r > 0
    chips = n_col // 2
    core, chip = lax.rem(me_c, 2), me_c // 2
    beside = me_c + 1 - 2 * core
    away = [lax.rem(chip + k, chips) * 2 + core for k in range(1, chips)]

    def greet(axis, to):
        pl.semaphore_signal(barrier, inc=1, device_id={axis: to}, device_id_type=MESH)

    pl.when(has_up)(lambda: greet("row", me_r + 1))
    pl.when(has_down)(lambda: greet("row", me_r - 1))
    for to in away + [beside]:
        greet("col", to)
    load_bias.wait()
    packed = bias_rows(bias_ref[...].astype(jnp.float32), width)
    cols[me_r, items : items + EXTRA, :] = packed
    rows[me_c, items : items + EXTRA, :] = packed
    load_counts.wait()
    for load in loads:
        load.wait()
    listed = bcount_ref[0, 0]

    def position(p, carry):
        bi, bj = p // n_cb, lax.rem(p, n_cb)
        slot = jnp.int32(0)
        found = jnp.int32(0)
        for s in range(slots):
            hit = jnp.logical_and(
                jnp.logical_and(brow_ref[0, 0, s] == bi, bcol_ref[0, 0, s] == bj), s < listed
            )
            slot = jnp.where(hit, s, slot)
            found = jnp.where(hit, 1, found)
        x = tally[slot] * found
        logged = jnp.log(jnp.maximum(x.astype(jnp.float32), 1.0))
        w = jnp.where(
            x > 0, jnp.minimum(1.0, jnp.exp(0.75 * (logged - jnp.log(jnp.float32(100.0))))), 0.0
        )
        at = pl.ds(pl.multiple_of(bi * side, side), side)
        weight[bj, at, :] = w
        logs[bj, at, :] = logged
        return carry


    load_emb.wait()
    load_own.wait()
    beyond = has_up.astype(jnp.int32) + has_down.astype(jnp.int32)
    pl.semaphore_wait(barrier, beyond + len(away) + 1)

    sent = []

    def send(src, dst, send_sem, recv_sem, axis, to, when=None):
        copy = pltpu.make_async_remote_copy(
            src_ref=src, dst_ref=dst, send_sem=send_sem, recv_sem=recv_sem,
            device_id={axis: to}, device_id_type=MESH,
        )
        if when is None:
            copy.start()
        else:
            pl.when(when)(copy.start)
        sent.append((copy, when))

    halves = (pl.ds(0, items // 2), pl.ds(items // 2, items - items // 2 + EXTRA))
    for h in range(2):
        mine = cols.at[me_r, halves[h]]
        send(mine, mine, cs_send.at[0, h], cs_recv.at[me_r, h], "row", me_r + 1, has_up)
        send(mine, mine, cs_send.at[1, h], cs_recv.at[me_r, h], "row", me_r - 1, has_down)
    mine = rows.at[me_c]
    for to in away:
        send(mine, mine, rs_send.at[to], rs_recv.at[me_c], "col", to)
    send(mine, mine, rs_send.at[beside], rs_recv.at[me_c], "col", beside)
    lax.fori_loop(0, n_rb * n_cb, position, 0)

    def arrived(buf, sem, axis, slot):
        pltpu.make_async_remote_copy(
            src_ref=buf.at[slot], dst_ref=buf.at[slot], send_sem=sem.at[slot],
            recv_sem=sem.at[slot], device_id={axis: slot}, device_id_type=MESH,
        ).wait_recv()

    def take(ms, when=None):
        for h in range(2):
            for m in ms:
                piece = cols.at[m, halves[h]]
                landed = pltpu.make_async_remote_copy(
                    src_ref=piece, dst_ref=piece, send_sem=cs_pass.at[m, h],
                    recv_sem=cs_recv.at[m, h], device_id={"row": m}, device_id_type=MESH,
                )
                if when is None:
                    landed.wait_recv()
                else:
                    pl.when(when)(landed.wait_recv)
                to = me_r + 2 * (m < me_r).astype(jnp.int32) - 1
                ok = jnp.logical_and(to >= 0, to < n_row)
                if when is not None:
                    ok = jnp.logical_and(ok, when)
                send(piece, piece, cs_pass.at[m, h], cs_recv.at[m, h], "row", to, ok)

    early = 2 if group == 1 and n_cb == 4 else 0
    inner = jnp.logical_and(has_up, has_down)
    if early:
        take([nearest(me_r, k, n_row) for k in range(1, early + 1)])
    for m in away:
        arrived(rows, rs_recv, "col", m)
        send(rows.at[m], rows.at[m], rs_pass.at[m], rs_recv.at[m], "col", beside)
    arrived(rows, rs_recv, "col", beside)
    for m in away:
        arrived(rows, rs_recv, "col", m + 1 - 2 * core)
    top = (lax.broadcasted_iota(jnp.int32, (EXTRA, side), 0) == 0).astype(jnp.float32).astype(jnp.bfloat16)
    for i in range(n_col):
        shift[i * items : (i + 1) * items, :] = lax.dot_general(
            rows[i, items : items + EXTRA, 0:items], top,
            (((0,), (0,)), ((), ())), preferred_element_type=jnp.float32,
        )

    all_rows = jnp.concatenate([rows[i, 0:items, :] for i in range(n_col)], axis=0)
    me_g = me_r // group
    for k in range(n_cb):
        jb = nearest(me_g, k, n_cb)
        if k == 0:
            members = [me_g * group + lax.rem(me_r + t, group) for t in range(1, group)]
        else:
            members = [jb * group + t for t in range(group)]
        if early and k == 1:
            take([nearest(me_r, early + 1, n_row)], inner)
        elif early and k == early + 1:
            take(members, jnp.logical_not(inner))
        elif not early:
            take(members)
        block = jnp.concatenate([cols[jb * group + t, 0:items, :] for t in range(group)], axis=0)
        cshift = jnp.concatenate(
            [cols[jb * group + t, items : items + EXTRA, 0:items].astype(jnp.float32)[0:1] for t in range(group)],
            axis=1,
        )
        scores = lax.dot_general(
            all_rows, block, (((1,), (1,)), ((), ())), preferred_element_type=jnp.float32
        )
        weighted = weight[jb] * (scores + shift[...] + cshift - logs[jb])
        rounded = weighted.astype(jnp.bfloat16)
        to_cols = lax.dot_general(
            rounded, all_rows, (((0,), (0,)), ((), ())), preferred_element_type=jnp.float32
        )
        sums = jnp.sum(weighted, axis=0, keepdims=True)
        if k == 0:
            wrow[...] = weighted
        else:
            wrow[...] += weighted
        for t in range(group):
            to = jb * group + t
            part = to_cols[t * items : (t + 1) * items]
            part_sums = sums[:, t * items : (t + 1) * items]
            col_out[to, 0:items, :] = part.astype(jnp.bfloat16)
            col_out[to, items : items + EXTRA, :] = bias_rows(part_sums, width)
            if k == 0:
                if group == 1:
                    col_own[0:items, :] = part
                    col_own[items : items + 1, 0:items] = part_sums
                else:

                    @pl.when(to == me_r)
                    def _():
                        col_own[0:items, :] = part
                        col_own[items : items + 1, 0:items] = part_sums
        for m in members:
            send(col_out.at[m], col_in.at[me_r], co_send.at[m], co_recv.at[me_r], "row", m)
        if k == n_cb - 1:
            last_w[...] = rounded
            last_block = block
        else:
            to_rows = jnp.dot(rounded, block, preferred_element_type=jnp.float32)
            if k == 0:
                racc[...] = to_rows
            else:
                racc[...] += to_rows

    def row_terms(at):
        return racc[at, :] + jnp.dot(
            last_w[at, :], last_block, preferred_element_type=jnp.float32
        )

    def row_sums(i):
        at = pl.ds(pl.multiple_of(i * items, items), items)
        return jnp.sum(jnp.transpose(wrow[at, :]), axis=0, keepdims=True)

    across = [a + t * (1 - 2 * core) for a in away for t in (0, 1)]
    for to in across + [beside]:
        at = pl.ds(pl.multiple_of(to * items, items), items)
        row_out[to, 0:items, :] = row_terms(at).astype(jnp.bfloat16)
        row_out[to, items : items + EXTRA, :] = bias_rows(row_sums(to), width)
        send(row_out.at[to], row_in.at[me_c], ro_send.at[to], ro_recv.at[me_c], "col", to)

    at = pl.ds(pl.multiple_of(me_c * items, items), items)
    total = row_terms(at) + col_own[0:items, :]
    btotal = row_sums(me_c) + col_own[items : items + 1, 0:items]

    def added(total, btotal, buf, slot):
        return (
            total + buf[slot, 0:items, :].astype(jnp.float32),
            btotal + buf[slot, items : items + EXTRA, 0:items].astype(jnp.float32)[0:1],
        )

    for k in range(1, n_col):
        slot = lax.rem(me_c + n_col - k, n_col)
        arrived(row_in, ro_recv, "col", slot)
        total, btotal = added(total, btotal, row_in, slot)
    for k in range(1, n_row):
        slot = nearest(me_r, k, n_row)
        arrived(col_in, co_recv, "row", slot)
        total, btotal = added(total, btotal, col_in, slot)
    grad_ref[...] = total * 0.0625
    gbias_ref[...] = btotal * 0.015625
    for copy, when in sent:
        if when is None:
            copy.wait_send()
        else:
            pl.when(when)(copy.wait_send)


def body(n_row, n_col, embedding, item_bias, counts, block_row, block_col, block_count):
    items, width = embedding.shape
    slots, side = counts.shape[2], counts.shape[3]
    span, across = n_col * items, n_row * items // side
    vmem = pl.BlockSpec(memory_space=pltpu.VMEM)
    smem = pl.BlockSpec(memory_space=pltpu.SMEM)
    hbm = pl.BlockSpec(memory_space=pltpu.HBM)
    tall = items + EXTRA
    dma = pltpu.SemaphoreType.DMA
    keep = lambda x: pltpu.with_memory_space_constraint(x, pltpu.HBM)
    grad, gbias = pl.pallas_call(
        functools.partial(kernel, n_row, n_col),
        out_shape=(
            jax.ShapeDtypeStruct((items, width), jnp.float32),
            jax.ShapeDtypeStruct((1, items), jnp.float32),
        ),
        in_specs=[hbm] * 6,
        out_specs=(vmem, vmem),
        scratch_shapes=[
            pltpu.SMEM((1, 1, slots), jnp.int32),
            pltpu.SMEM((1, 1, slots), jnp.int32),
            pltpu.SMEM((1, 1), jnp.int32),
            pltpu.VMEM((1, items), jnp.bfloat16),
            pltpu.VMEM((n_col, tall, width), jnp.bfloat16),
            pltpu.VMEM((n_row, tall, width), jnp.bfloat16),
            pltpu.VMEM((slots, side, side), jnp.int32),
            pltpu.VMEM((across, span, side), jnp.float32),
            pltpu.VMEM((across, span, side), jnp.float32),
            pltpu.VMEM((span, side), jnp.float32),
            pltpu.VMEM((span, side), jnp.float32),
            pltpu.VMEM((span, width), jnp.float32),
            pltpu.VMEM((n_col, tall, width), jnp.bfloat16),
            pltpu.VMEM((n_row, tall, width), jnp.bfloat16),
            pltpu.VMEM((n_col, tall, width), jnp.bfloat16),
            pltpu.VMEM((n_row, tall, width), jnp.bfloat16),
            pltpu.VMEM((items + 8, width), jnp.float32),
            dma((7,)),
            dma((n_col,)), dma((n_col,)),
            dma((2, 2)), dma((n_row, 2)),
            dma((n_col,)), dma((n_col,)),
            dma((n_row,)), dma((n_row,)),
            dma((n_col,)), dma((n_row, 2)),
            pltpu.VMEM((span, side), jnp.bfloat16),
        ],
        compiler_params=pltpu.CompilerParams(
            collective_id=0, has_side_effects=True, vmem_limit_bytes=48 << 20
        ),
    )(
        keep(embedding), keep(item_bias.reshape(1, items)), keep(counts),
        block_row, block_col, block_count,
    )
    return grad, gbias.reshape(items)


PIECES = 4


def line_kernel(
    emb_hbm, bias_hbm, counts_hbm, brow_hbm, bcol_hbm, bcount_hbm,
    grad_ref, gbias_ref,
    brow_ref, bcol_ref, bcount_ref, bias_ref, rows, cols, row_bias, col_bias, tally, weight, logs, shift, wrow, wbuf, racc,
    col_out, col_in, relay, row_out, row_in, csum_out, csum_in, rsum_out, rsum_in,
    load_sem, e_send, e_pass, e_recv, eb_send, eb_pass, eb_recv, r_send, r_pass, r_recv, rb_send, rb_pass, rb_recv,
    co_send, co_recv, relay_send, relay_recv, ro_send, ro_recv, cs_send, cs_recv, rs_send, rs_recv,
):
    items, width = emb_hbm.shape
    slots, side = counts_hbm.shape[2], counts_hbm.shape[3]
    n_row, n_col = cols.shape[0], rows.shape[0] // items
    piece = items // PIECES
    me_r, me_c = lax.axis_index("row"), lax.axis_index("col")
    mate, opp, mir = me_r + 1 - 2 * lax.rem(me_r, 2), lax.rem(me_r + 2, n_row), n_row - 1 - me_r
    end = jnp.logical_or(me_r == 0, me_r == n_row - 1)
    inner = jnp.logical_not(end)
    core = lax.rem(me_c, 2)
    beside, across = me_c + 1 - 2 * core, lax.rem(me_c + 2, n_col)
    diag = across + 1 - 2 * core

    def part(i):
        return pl.ds(i * piece, piece)

    def row_at(m, i=0, height=items):
        return pl.ds(pl.multiple_of(m * items + i * piece, piece), height)

    load_bias = pltpu.make_async_copy(bias_hbm, bias_ref, load_sem.at[0])
    load_emb = pltpu.make_async_copy(emb_hbm, cols.at[me_r], load_sem.at[1])
    load_own = pltpu.make_async_copy(emb_hbm, rows.at[row_at(me_c)], load_sem.at[2])
    load_lists = [
        pltpu.make_async_copy(src, dst, load_sem.at[3 + i])
        for i, (src, dst) in enumerate(((brow_hbm, brow_ref), (bcol_hbm, bcol_ref), (bcount_hbm, bcount_ref)))
    ]
    load_counts = pltpu.make_async_copy(counts_hbm.at[0, 0], tally, load_sem.at[6])
    for load in [load_emb, load_own, load_bias] + load_lists + [load_counts]:
        load.start()

    barrier = pltpu.get_barrier_semaphore()

    def greet(axis, to):
        pl.semaphore_signal(barrier, inc=1, device_id={axis: to}, device_id_type=MESH)

    greet("row", mate)
    pl.when(inner)(lambda: greet("row", mir))
    greet("col", across)
    greet("col", beside)

    load_bias.wait()
    own_bias = jnp.broadcast_to(bias_ref[...].astype(jnp.float32), (EXTRA, items))
    row_bias[me_c] = own_bias
    col_bias[me_r] = own_bias
    load_emb.wait()
    load_own.wait()
    pl.semaphore_wait(barrier, 3 + inner.astype(jnp.int32))

    sent = []

    def remote(src, dst, send_sem, recv_sem, axis, to):
        return pltpu.make_async_remote_copy(
            src_ref=src, dst_ref=dst, send_sem=send_sem, recv_sem=recv_sem,
            device_id={axis: to}, device_id_type=MESH,
        )

    def send(src, dst, send_sem, recv_sem, axis, to, when=None):
        copy = remote(src, dst, send_sem, recv_sem, axis, to)
        if when is None:
            copy.start()
        else:
            pl.when(when)(copy.start)
        sent.append((copy, when))

    def landed(dst, recv_sem, axis):
        remote(dst, dst, recv_sem, recv_sem, axis, me_r if axis == "row" else me_c).wait_recv()

    def drain(copies):
        for group, when in ((None, None), (end, end), (inner, inner)):
            these = [copy for copy, w in copies if w is group]
            if when is None:
                for copy in these:
                    copy.wait_send()
            elif these:

                @pl.when(when)
                def _():
                    for copy in these:
                        copy.wait_send()

    own = col_bias.at[me_r]
    send(own, own, eb_send.at[0], eb_recv.at[me_r], "row", mate)
    send(own, own, eb_send.at[1], eb_recv.at[me_r], "row", mir, inner)
    own = row_bias.at[me_c]
    send(own, own, rb_send.at[0], rb_recv.at[me_c], "col", across)
    send(own, own, rb_send.at[1], rb_recv.at[me_c], "col", beside)

    for i in range(PIECES):
        own = cols.at[me_r, part(i)]
        send(own, own, e_send.at[0, i], e_recv.at[me_r, i], "row", mate)
        send(own, own, e_send.at[1, i], e_recv.at[me_r, i], "row", mir, inner)
        own = rows.at[row_at(me_c, i, piece)]
        send(own, own, r_send.at[i], r_recv.at[me_c, i], "col", across)
    own = rows.at[row_at(me_c)]
    send(own, own, r_send.at[PIECES], r_recv.at[me_c, 0], "col", beside)

    for load in load_lists + [load_counts]:
        load.wait()
    listed = bcount_ref[0, 0]
    code = [
        jnp.where(s < listed, brow_ref[0, 0, s] * n_row + bcol_ref[0, 0, s], -1) for s in range(slots)
    ]

    def position(p, carry):
        bi, bj = p // n_row, lax.rem(p, n_row)
        slot = jnp.int32(0)
        found = jnp.int32(0)
        for s in range(slots):
            hit = code[s] == p
            slot = jnp.where(hit, s, slot)
            found = jnp.where(hit, 1, found)
        x = tally[slot] * found
        logged = jnp.log(jnp.maximum(x.astype(jnp.float32), 1.0))
        w = jnp.where(
            x > 0, jnp.minimum(1.0, jnp.exp(0.75 * (logged - jnp.log(jnp.float32(100.0))))), 0.0
        )
        at = pl.ds(pl.multiple_of(bi * side, side), side)
        weight[bj, at, :] = w
        logs[bj, at, :] = logged
        return carry

    lax.fori_loop(0, n_col * n_row, position, 0)

    def came(m, i):
        landed(cols.at[m, part(i)], e_recv.at[m, i], "row")

    def hand(m, i, to):
        return remote(
            cols.at[m, part(i)], cols.at[m, part(i)], e_pass.at[m, i], e_recv.at[m, i], "row", to
        )

    def bias_came(m):
        landed(col_bias.at[m], eb_recv.at[m], "row")

    def bias_hand(m, to):
        return remote(col_bias.at[m], col_bias.at[m], eb_pass.at[m], eb_recv.at[m], "row", to)

    def later(copy, when):
        sent.append((copy, when))
        return copy

    outward = [[later(hand(m, i, mate), inner) for i in range(PIECES)] for m in (mir, opp)]
    inward = [later(hand(mate, i, mir), inner) for i in range(PIECES)]
    bias_outward = [later(bias_hand(m, mate), inner) for m in (mir, opp)]
    bias_inward = later(bias_hand(mate, mir), inner)
    to_relay = [
        [
            later(remote(col_out.at[m, part(i)], relay.at[k, part(i)], relay_send.at[k, i], relay_recv.at[k, i], "row", mate), end)
            for i in range(PIECES)
        ]
        for k, m in enumerate((opp, mir))
    ]
    from_relay = [
        [
            later(remote(col_out.at[m, part(i)], col_in.at[me_r, part(i)], co_send.at[m, i], co_recv.at[me_r, i], "row", m), inner)
            for i in range(PIECES)
        ]
        for m in (mir, opp)
    ]

    for i in range(PIECES):
        came(mate, i)
        if i == 0:
            bias_came(mate)

        @pl.when(inner)
        def _():
            if i == 0:
                bias_inward.start()
            inward[i].start()
            came(mir, i)
            if i == 0:
                bias_came(mir)
                bias_outward[0].start()
            outward[0][i].start()

        if i == 0:
            landed(row_bias.at[across], rb_recv.at[across], "col")
            send(row_bias.at[across], row_bias.at[across], rb_pass.at[0], rb_recv.at[across], "col", beside)
        landed(rows.at[row_at(across, i, piece)], r_recv.at[across, i], "col")
        passed = rows.at[row_at(across, i, piece)]
        send(passed, passed, r_pass.at[i], r_recv.at[across, i], "col", beside)

    landed(rows.at[row_at(beside)], r_recv.at[beside, 0], "col")
    landed(row_bias.at[beside], rb_recv.at[beside], "col")
    for i in range(PIECES):
        landed(rows.at[row_at(diag, i, piece)], r_recv.at[diag, i], "col")
    landed(row_bias.at[diag], rb_recv.at[diag], "col")

    top = (lax.broadcasted_iota(jnp.int32, (EXTRA, side), 0) == 0).astype(jnp.float32).astype(jnp.bfloat16)
    for m in range(n_col):
        shift[m * items : (m + 1) * items, :] = lax.dot_general(
            row_bias[m].astype(jnp.bfloat16), top,
            (((0,), (0,)), ((), ())), preferred_element_type=jnp.float32,
        )

    pick = lambda a, b: jnp.where(end, a, b)
    order = [mate, pick(me_r, mir), pick(opp, me_r), pick(mir, opp)]

    def residual(k):
        m = order[k]
        scores = lax.dot_general(
            rows[...], cols[m], (((1,), (1,)), ((), ())), preferred_element_type=jnp.float32
        )
        weighted = weight[m] * (scores + shift[...] + col_bias[m, 0:1, :] - logs[m])
        wbuf[k] = weighted.astype(jnp.bfloat16)
        if k == 0:
            wrow[...] = weighted
        else:
            wrow[...] += weighted
        csum_out[m] = jnp.broadcast_to(jnp.sum(weighted, axis=0, keepdims=True), (EXTRA, side))

    def to_cols(k):
        col_out[order[k]] = lax.dot_general(
            wbuf[k], rows[...], (((0,), (0,)), ((), ())), preferred_element_type=jnp.float32
        ).astype(jnp.bfloat16)

    def send_col(k, when=None):
        m = order[k]
        send(col_out.at[m], col_in.at[me_r], co_send.at[m, 0], co_recv.at[me_r, 0], "row", m, when)

    def send_csum(k, when=None):
        m = order[k]
        send(csum_out.at[m], csum_in.at[me_r], cs_send.at[m], cs_recv.at[me_r], "row", m, when)

    def relay_e(pieces):
        for i in pieces:
            came(opp, i)
            outward[1][i].start()

    residual(0)
    to_cols(0)
    send_col(0, end)
    send_csum(0)
    @pl.when(inner)
    def _():
        bias_came(opp)
        bias_outward[1].start()
        relay_e((0, 1))


    residual(1)
    to_cols(1)
    send_csum(1, inner)
    pl.when(inner)(lambda: relay_e((2,)))

    @pl.when(end)
    def _():
        for i in range(PIECES):
            came(opp, i)
        bias_came(opp)

    residual(2)
    to_cols(2)
    send_csum(2, end)

    racc[...] = jnp.dot(
        jnp.concatenate([wbuf[0], wbuf[1]], axis=1),
        jnp.concatenate([cols[order[0]], cols[order[1]]], axis=0),
        preferred_element_type=jnp.float32,
    )

    @pl.when(inner)
    def _():
        relay_e((3,))

    send_col(0, inner)

    groups = ((0, 2), (2, 3))
    begun = groups[-1][1]

    @pl.when(end)
    def _():
        bias_came(mir)
        for a, b in groups:
            for i in range(a, b):
                came(mir, i)
            some = [jnp.zeros((n * piece, width), jnp.bfloat16) for n in (a, PIECES - b)]
            some = [some[0]] * (a > 0) + [cols[mir, a * piece : b * piece, :]] + [some[1]] * (b < PIECES)
            scores = lax.dot_general(
                rows[...], jnp.concatenate(some, axis=0), (((1,), (1,)), ((), ())), preferred_element_type=jnp.float32
            )
            weighted = weight[mir] * (scores + shift[...] + col_bias[mir, 0:1, :] - logs[mir])
            col_out[mir, a * piece : b * piece, :] = lax.dot_general(
                weighted.astype(jnp.bfloat16), rows[...], (((0,), (0,)), ((), ())), preferred_element_type=jnp.float32
            )[a * piece : b * piece].astype(jnp.bfloat16)
            for i in range(a, b):
                to_relay[1][i].start()
        for i in range(begun, PIECES):
            came(mir, i)

    residual(3)
    pair = jnp.concatenate([cols[order[2]], cols[order[3]]], axis=0)

    def row_terms(m):
        at = row_at(m)
        left = jnp.concatenate([wbuf[2, at, :], wbuf[3, at, :]], axis=1)
        return racc[at, :] + jnp.dot(left, pair, preferred_element_type=jnp.float32)

    def row_sums(m):
        return jnp.sum(jnp.transpose(wrow[row_at(m), :]), axis=0, keepdims=True)

    row_out[0] = row_terms(diag).astype(jnp.bfloat16)
    send(row_out.at[0], row_in.at[0], ro_send.at[0], ro_recv.at[0], "col", beside)
    columns = lax.dot_general(
        wbuf[3], rows[...], (((0,), (0,)), ((), ())), preferred_element_type=jnp.float32
    ).astype(jnp.bfloat16)
    col_out[order[3], begun * piece :, :] = columns[begun * piece :]

    @pl.when(end)
    def _():
        for i in range(begun, PIECES):
            to_relay[1][i].start()

    @pl.when(inner)
    def _():
        col_out[opp, : begun * piece, :] = columns[: begun * piece]


    @pl.when(end)
    def _():
        for copy in to_relay[0]:
            copy.start()

    send_csum(3)
    row_out[1] = row_terms(beside).astype(jnp.bfloat16)
    send(row_out.at[1], row_in.at[1], ro_send.at[1], ro_recv.at[1], "col", beside)

    mine = row_terms(across)
    early = [(c, w) for c, w in sent if not any(c is d for d in to_relay[0] + to_relay[1] + from_relay[0] + from_relay[1])]
    landed(row_in.at[0], ro_recv.at[0], "col")
    row_out[2] = (mine + row_in[0].astype(jnp.float32)).astype(jnp.bfloat16)
    send(row_out.at[2], row_in.at[2], ro_send.at[2], ro_recv.at[2], "col", across)
    for m in (diag, across, beside):
        rsum_out[m] = jnp.broadcast_to(row_sums(m), (EXTRA, items))
        send(rsum_out.at[m], rsum_in.at[me_c], rs_send.at[m], rs_recv.at[me_c], "col", m)
    grad_ref[...] = row_terms(me_c) + col_out[me_r].astype(jnp.float32)
    btotal = row_sums(me_c) + csum_out[me_r, 0:1, :]
    late = [(c, w) for c, w in sent if not any(c is d for d, _ in early)]

    @pl.when(inner)
    def _():
        for k, m in ((1, opp), (0, mir)):
            for i in range(PIECES):
                landed(relay.at[k, part(i)], relay_recv.at[k, i], "row")
                col_out[m, part(i), :] = (
                    col_out[m, part(i), :].astype(jnp.float32) + relay[k, part(i), :].astype(jnp.float32)
                ).astype(jnp.bfloat16)
                from_relay[k][i].start()

    drain(early)
    landed(row_in.at[1], ro_recv.at[1], "col")
    landed(col_in.at[mate], co_recv.at[mate, 0], "row")
    grad_ref[...] += row_in[1].astype(jnp.float32) + col_in[mate].astype(jnp.float32)
    for m in (mate, opp, mir):
        landed(csum_in.at[m], cs_recv.at[m], "row")
        btotal += csum_in[m, 0:1, :]
    for m in (beside, across, diag):
        landed(rsum_in.at[m], rs_recv.at[m], "col")
        btotal += rsum_in[m, 0:1, :]
    gbias_ref[...] = btotal * 0.015625
    landed(row_in.at[2], ro_recv.at[2], "col")
    grad_ref[...] += row_in[2].astype(jnp.float32)

    last = pick(opp, mir)
    for i in range(PIECES):
        landed(col_in.at[last, part(i)], co_recv.at[last, i], "row")
        grad_ref[part(i), :] = (
            grad_ref[part(i), :] + col_in[last, part(i), :].astype(jnp.float32)
        ) * 0.0625
    drain(late)


def line_body(n_row, n_col, embedding, item_bias, counts, block_row, block_col, block_count):
    items, width = embedding.shape
    slots, side = counts.shape[2], counts.shape[3]
    span = n_col * items
    bf16, f32 = jnp.bfloat16, jnp.float32
    vmem = pl.BlockSpec(memory_space=pltpu.VMEM)
    hbm = pl.BlockSpec(memory_space=pltpu.HBM)
    dma = pltpu.SemaphoreType.DMA
    keep = lambda x: pltpu.with_memory_space_constraint(x, pltpu.HBM)
    grad, gbias = pl.pallas_call(
        line_kernel,
        out_shape=(
            jax.ShapeDtypeStruct((items, width), f32),
            jax.ShapeDtypeStruct((1, items), f32),
        ),
        in_specs=[hbm] * 6,
        out_specs=(vmem, vmem),
        scratch_shapes=[
            pltpu.SMEM((1, 1, slots), jnp.int32),
            pltpu.SMEM((1, 1, slots), jnp.int32),
            pltpu.SMEM((1, 1), jnp.int32),
            pltpu.VMEM((1, items), bf16),
            pltpu.VMEM((span, width), bf16),
            pltpu.VMEM((n_row, items, width), bf16),
            pltpu.VMEM((n_col, EXTRA, items), f32),
            pltpu.VMEM((n_row, EXTRA, items), f32),
            pltpu.VMEM((slots, side, side), jnp.int32),
            pltpu.VMEM((n_row, span, side), f32),
            pltpu.VMEM((n_row, span, side), f32),
            pltpu.VMEM((span, side), f32),
            pltpu.VMEM((span, side), f32),
            pltpu.VMEM((n_row, span, side), bf16),
            pltpu.VMEM((span, width), f32),
            pltpu.VMEM((n_row, items, width), bf16),
            pltpu.VMEM((n_row, items, width), bf16),
            pltpu.VMEM((2, items, width), bf16),
            pltpu.VMEM((3, items, width), bf16),
            pltpu.VMEM((3, items, width), bf16),
            pltpu.VMEM((n_row, EXTRA, items), f32),
            pltpu.VMEM((n_row, EXTRA, items), f32),
            pltpu.VMEM((n_col, EXTRA, items), f32),
            pltpu.VMEM((n_col, EXTRA, items), f32),
            dma((7,)),
            dma((2, PIECES)), dma((n_row, PIECES)), dma((n_row, PIECES)),
            dma((2,)), dma((n_row,)), dma((n_row,)),
            dma((PIECES + 1,)), dma((PIECES,)), dma((n_col, PIECES)),
            dma((2,)), dma((1,)), dma((n_col,)),
            dma((n_row, PIECES)), dma((n_row, PIECES)),
            dma((2, PIECES)), dma((2, PIECES)),
            dma((3,)), dma((3,)),
            dma((n_row,)), dma((n_row,)),
            dma((n_col,)), dma((n_col,)),
        ],
        compiler_params=pltpu.CompilerParams(
            collective_id=0, has_side_effects=True, vmem_limit_bytes=48 << 20
        ),
    )(
        keep(embedding), keep(item_bias.reshape(1, items)), keep(counts),
        keep(block_row), keep(block_col), block_count,
    )
    return grad, gbias.reshape(items)


def solution(mesh):
    placed = (
        P(("grp", "row", "col"), None),
        P(("grp", "row", "col")),
        P(("grp", "row"), "col", None, None, None),
        P(("grp", "row"), "col", None),
        P(("grp", "row"), "col", None),
        P(("grp", "row"), "col"),
    )

    def either(*args):
        n_row, n_col = mesh.shape["row"], mesh.shape["col"]
        line = n_row == 4 and n_col == 4 and args[0].shape[0] == args[2].shape[3]
        return (line_body if line else body)(n_row, n_col, *args)

    return jax.shard_map(
        either,
        mesh=mesh,
        in_specs=placed,
        out_specs=(P(("grp", "row", "col"), None), P(("grp", "row", "col"))),
        check_vma=False,
    )
```
